32 devices in a mesh: ctx: 8 (over y, x, core), head: 4 (over z).
Axes of the slice: x: 2, y: 2, z: 4, core: 2. Of those that a mesh axis runs over, the one named last changes fastest.
Arguments:
- input_queries: bfloat16 [8192, 6144], P(('ctx', 'head')), may hold values from -6 to 6
- input_keys: bfloat16 [8192, 1024], P(('ctx', 'head')), may hold values from -6 to 6
- input_values: bfloat16 [8192, 1024], P(('ctx', 'head')), may hold values from -6 to 6
- cotangent: bfloat16 [8192, 6144], P(('ctx', 'head')), may hold values from -6 to 6
- block_list: int32 [16, 8], replicated, may hold values from 0 to 15, as said below
- block_count: int32 [16], replicated, may hold values from 1 to 8, as said below
Outputs:
- attn_out: bfloat16 [8192, 6144], P(('ctx', 'head'))
- grad_query: bfloat16 [8192, 6144], P(('ctx', 'head'))
- key_gradient: bfloat16 [8192, 1024], P(('ctx', 'head'))
- value_gradient: bfloat16 [8192, 1024], P(('ctx', 'head'))
The draws below stay inside these ranges and needn't reach their ends.
Inputs may be any that keep to these rules, and one draw needn't show every extreme that they name: `block_list`: row b lists entry 0 = b itself, then distinct blocks of other ctx indices up to position block_count[b] - 1, block c belonging to ctx index c // 2; entries from position block_count[b] on repeat b and are unused. The rows of the 2 query blocks of one ctx index together name at most one block of any other ctx index. `block_count`: query block 0 lists 8 blocks.
All inputs are finite; a program needn't handle non-finite values.
Results may differ from the reference program's by a relative error of at most 0.015.
Values may be sent and summed in bfloat16 or wider, within the bound.
No kernel may reach another device: no remote copies, remote signals or barrier semaphores. Data moves between devices by JAX's collectives and lax.ppermute only.
A program may use at most 128 MiB of HBM per device.

```python
import jax
import jax.numpy as jnp
from jax import lax

QUERY_HEADS = 48
KEY_VALUE_HEADS = 8
HEAD_WIDTH = 128
BLOCK_TOKENS = 512
MOST_KEY_BLOCKS = 8
QBLK_DEV = 2
SEQUENCE_BLOCKS = 16
SEQUENCE_TOKENS = 8192


def draw_input_keys(key, part):
    return jax.random.truncated_normal(jax.random.fold_in(key, 21), -6.0, 6.0, (SEQUENCE_TOKENS, KEY_VALUE_HEADS * HEAD_WIDTH), jnp.float32).astype(jnp.bfloat16)


def draw_input_queries(key, part):
    return jax.random.truncated_normal(jax.random.fold_in(key, 22), -6.0, 6.0, (SEQUENCE_TOKENS, QUERY_HEADS * HEAD_WIDTH), jnp.float32).astype(jnp.bfloat16)


def plan_lists(key):
    starting_key = jax.random.fold_in(key, 505)
    owner_total = SEQUENCE_BLOCKS // QBLK_DEV
    device_of = jnp.arange(SEQUENCE_BLOCKS) // QBLK_DEV
    load_level = jax.random.randint(jax.random.fold_in(starting_key, 1), (owner_total,), 0, 4)
    extra_span = 1 + 3 * load_level[device_of]
    extra_blocks = jnp.minimum(jax.random.randint(jax.random.fold_in(starting_key, 2), (SEQUENCE_BLOCKS,), 0, 2520) % extra_span, MOST_KEY_BLOCKS - 1)
    extra_blocks = extra_blocks.at[0].set(MOST_KEY_BLOCKS - 1)
    live_count = (1 + extra_blocks).astype(jnp.int32)
    chosen = jnp.arange(owner_total)[None, :] * QBLK_DEV + jax.random.randint(jax.random.fold_in(starting_key, 3), (owner_total, owner_total), 0, QBLK_DEV)
    order_key = jax.random.randint(jax.random.fold_in(starting_key, 4), (SEQUENCE_BLOCKS, owner_total), 0, 1 << 20) * owner_total + jnp.arange(owner_total)[None, :]
    order_key = jnp.where(jnp.arange(owner_total)[None, :] == device_of[:, None], 1 << 30, order_key)
    owner_order = jnp.argsort(order_key, axis=1)
    remote = owner_order[:, :MOST_KEY_BLOCKS - 1]
    picked = chosen[device_of[:, None], remote]
    slot_index = jnp.arange(1, MOST_KEY_BLOCKS)[None, :]
    tail_entries = jnp.where(slot_index < live_count[:, None], picked, jnp.arange(SEQUENCE_BLOCKS)[:, None])
    list_rows = jnp.concatenate([jnp.arange(SEQUENCE_BLOCKS)[:, None], tail_entries], axis=1).astype(jnp.int32)
    return (list_rows, live_count)


def draw_block_list(key, part):
    return plan_lists(key)[0]


def draw_block_count(key, part):
    return plan_lists(key)[1]


def block_levels(own_key, extent, shards, low, high):
    def one(position, blocks):
        draws = jax.random.uniform(jax.random.fold_in(jax.random.fold_in(own_key, 6), position), (blocks,), jnp.float32, low / len(shards), high / len(shards))
        return jnp.repeat(jnp.exp(draws), extent[position] // blocks).reshape((-1,) + (1,) * (len(extent) - position - 1))

    factor_of = one(*shards[0])
    for cut in shards[1:]:
        factor_of = factor_of * one(*cut)
    return factor_of


def gaussian(own_key, shape, scale, bound, shards=(), held_as=jnp.bfloat16):
    drawn = jax.random.normal(own_key, shape, jnp.float32) * scale
    if len(shards) > 0:
        drawn = block_levels(own_key, shape, shards, -0.22, 0.18) * drawn
    return jnp.clip(drawn, min=-bound, max=bound).astype(held_as)


def setup_inputs(seed: int = 0) -> dict:
    arg_keys = jax.random.split(jax.random.key(seed), 7)
    return {
        "input_queries": draw_input_queries(jax.random.fold_in(arg_keys[6], 71), 0),
        "input_keys": draw_input_keys(jax.random.fold_in(arg_keys[6], 71), 0),
        "input_values": gaussian(arg_keys[2], (SEQUENCE_TOKENS, KEY_VALUE_HEADS * HEAD_WIDTH), 1.0, 6.0, ((0, 32),)),
        "cotangent": gaussian(arg_keys[3], (SEQUENCE_TOKENS, QUERY_HEADS * HEAD_WIDTH), 1.0, 6.0, ((0, 32),)),
        "block_list": draw_block_list(jax.random.fold_in(arg_keys[6], 71), 0),
        "block_count": draw_block_count(jax.random.fold_in(arg_keys[6], 71), 0),
    }


NEG_FILL = -1.0e30


def round_trip(values):
    return lax.optimization_barrier(values.astype(jnp.bfloat16)).astype(jnp.float32)


def reference(input_queries, input_keys, input_values, cotangent, block_list, block_count):
    group_width = QUERY_HEADS // KEY_VALUE_HEADS
    score_scale = HEAD_WIDTH ** -0.5
    blocked_queries = input_queries.reshape(SEQUENCE_BLOCKS, BLOCK_TOKENS, KEY_VALUE_HEADS, group_width, HEAD_WIDTH)
    cotangent_blocks = cotangent.reshape(SEQUENCE_BLOCKS, BLOCK_TOKENS, KEY_VALUE_HEADS, group_width, HEAD_WIDTH)
    blocked_keys = input_keys.reshape(SEQUENCE_BLOCKS, BLOCK_TOKENS, KEY_VALUE_HEADS, HEAD_WIDTH)
    blocked_values = input_values.reshape(SEQUENCE_BLOCKS, BLOCK_TOKENS, KEY_VALUE_HEADS, HEAD_WIDTH)

    def one_block(block_tables, inputs):
        key_table, value_table = block_tables
        query_b, cot_b, table_entries, live_count = inputs
        live_keys = jnp.repeat(jnp.arange(MOST_KEY_BLOCKS) < live_count, BLOCK_TOKENS)
        selected_keys = blocked_keys[table_entries].reshape(MOST_KEY_BLOCKS * BLOCK_TOKENS, KEY_VALUE_HEADS, HEAD_WIDTH)
        selected_values = blocked_values[table_entries].reshape(MOST_KEY_BLOCKS * BLOCK_TOKENS, KEY_VALUE_HEADS, HEAD_WIDTH)

        def one_head(operands):
            query_head, cot_head, key_head, value_head = operands
            query_f = query_head.astype(jnp.float32)
            cot_f = cot_head.astype(jnp.float32)
            key_f = key_head.astype(jnp.float32)
            value_f = value_head.astype(jnp.float32)
            scores = jnp.einsum("qjd,kd->jqk", query_f, key_f) * score_scale
            scores = jnp.where(live_keys[None, None, :], scores, NEG_FILL)
            top_score = jnp.max(scores, axis=-1, keepdims=True)
            log_total = top_score + jnp.log(jnp.sum(jnp.exp(scores - top_score), axis=-1, keepdims=True))
            weights = jnp.where(live_keys[None, None, :], jnp.exp(scores - log_total), 0.0)
            weights_b = round_trip(weights)
            attended = lax.optimization_barrier(jnp.einsum("jqk,kd->qjd", weights_b, value_f).astype(jnp.bfloat16))
            row_delta = jnp.sum(attended.astype(jnp.float32) * cot_f, axis=-1)
            grad_weights = jnp.einsum("qjd,kd->jqk", cot_f, value_f)
            grad_scores = round_trip(weights * (grad_weights - row_delta.T[:, :, None]))
            grad_q = (score_scale * jnp.einsum("jqk,kd->qjd", grad_scores, key_f)).astype(jnp.bfloat16)
            key_gradient_part = score_scale * jnp.einsum("jqk,qjd->kd", grad_scores, query_f)
            value_gradient_part = jnp.einsum("jqk,qjd->kd", weights_b, cot_f)
            return attended, grad_q, key_gradient_part, value_gradient_part

        attended, grad_q, key_gradient_part, value_gradient_part = lax.map(one_head, (jnp.moveaxis(query_b, 1, 0), jnp.moveaxis(cot_b, 1, 0), jnp.moveaxis(selected_keys, 1, 0), jnp.moveaxis(selected_values, 1, 0)))
        key_gradient_part = jnp.transpose(key_gradient_part.reshape(KEY_VALUE_HEADS, MOST_KEY_BLOCKS, BLOCK_TOKENS, HEAD_WIDTH), (1, 2, 0, 3))
        value_gradient_part = jnp.transpose(value_gradient_part.reshape(KEY_VALUE_HEADS, MOST_KEY_BLOCKS, BLOCK_TOKENS, HEAD_WIDTH), (1, 2, 0, 3))
        key_table = key_table.at[table_entries].add(key_gradient_part)
        value_table = value_table.at[table_entries].add(value_gradient_part)
        return (key_table, value_table), (jnp.moveaxis(attended, 0, 1), jnp.moveaxis(grad_q, 0, 1))

    empty_table = jnp.zeros((SEQUENCE_BLOCKS, BLOCK_TOKENS, KEY_VALUE_HEADS, HEAD_WIDTH), jnp.float32)
    block_tables, outputs = lax.scan(one_block, (empty_table, empty_table), (blocked_queries, cotangent_blocks, block_list, block_count))
    attn_out = outputs[0].reshape(SEQUENCE_TOKENS, QUERY_HEADS * HEAD_WIDTH)
    grad_query = outputs[1].reshape(SEQUENCE_TOKENS, QUERY_HEADS * HEAD_WIDTH)
    key_gradient = block_tables[0].reshape(SEQUENCE_TOKENS, KEY_VALUE_HEADS * HEAD_WIDTH).astype(jnp.bfloat16)
    value_gradient = block_tables[1].reshape(SEQUENCE_TOKENS, KEY_VALUE_HEADS * HEAD_WIDTH).astype(jnp.bfloat16)
    return attn_out, grad_query, key_gradient, value_gradient
```

```python
import functools
import math

import jax
import jax.numpy as jnp
from jax import lax
from jax.experimental import pallas as pl
from jax.experimental.pallas import tpu as pltpu
from jax.sharding import PartitionSpec as P

QUERY_HEADS = 48
KEY_VALUE_HEADS = 8
HEAD_WIDTH = 128
BLOCK_TOKENS = 512
GROUP_WIDTH = QUERY_HEADS // KEY_VALUE_HEADS

CHUNKS = (2, 2, 2)

SCORE_SCALE = HEAD_WIDTH ** (-0.5)
EXP2_SCALE = SCORE_SCALE * math.log2(math.e)
LOWEST = -3.0e38
VMEM_BYTES = 60 * 1024 * 1024


NT = (((1,), (1,)), ((), ()))
NN = (((1,), (0,)), ((), ()))
TN = (((0,), (0,)), ((), ()))


def dot(a, b, dims):
    return lax.dot_general(a, b, dims, preferred_element_type=jnp.float32)


def run_copies(copies):
    for copy in copies:
        copy.start()
    for copy in copies:
        copy.wait()


class Layout:
    def __init__(self, ctx_size, head_size, tokens):
        self.heads = head_size
        self.subs = KEY_VALUE_HEADS // head_size
        self.areas = ctx_size // self.subs
        self.group = KEY_VALUE_HEADS
        self.tokens = tokens
        self.ctx_size = ctx_size
        self.blocks_per_ctx = tokens * head_size // BLOCK_TOKENS
        self.own_blocks = self.blocks_per_ctx * self.subs
        self.blocks = self.own_blocks * self.areas
        self.table = self.group * tokens
        self.relay = head_size == 4

    def column(self, x, u):
        xr, xh = divmod(x, self.heads)
        return jnp.bitwise_xor(u, xh * self.subs + xr)

    def permute(self, value, xa=0, xr=0, xh=0):
        pairs = []
        for ctx in range(self.ctx_size):
            other = ctx ^ (xa * self.subs + xr)
            for head in range(self.heads):
                pairs.append((ctx * self.heads + head, other * self.heads + (head ^ xh)))
        return lax.ppermute(value, ("ctx", "head"), pairs)

    def exchange(self, slabs):
        got = [slabs[0]] + [None] * (self.group - 1)
        late = []
        order = sorted(range(1, self.group), key=lambda x: (x % self.heads == 0, x % self.heads != 2))
        for x in order:
            xr, xh = divmod(x, self.heads)
            if self.relay and xh == 2:
                first, second = (1, 3) if xr == 0 else (3, 1)
                late.append((x, self.permute(slabs[x], xr=xr, xh=first), second))
            else:
                got[x] = self.permute(slabs[x], xr=xr, xh=xh)
        for x, value, second in late:
            got[x] = self.permute(value, xh=second)
        return got


def pack_kernel(lay, chunks, with_kv, u_ref, *refs):
    n_in = 4 if with_kv else 2
    ins, refs = refs[:n_in], refs[n_in:]
    n_out = lay.group * (len(chunks) + (1 if with_kv else 0))
    outs, sems = refs[:n_out], refs[n_out]
    u = u_ref[0]
    copies = []

    def add(src, dst):
        copies.append(pltpu.make_async_copy(src, dst, sems.at[len(copies)]))

    at = 0
    if with_kv:
        for x in range(lay.group):
            col = pl.multiple_of(lay.column(x, u) * HEAD_WIDTH, HEAD_WIDTH)
            for half in range(2):
                add(ins[2 + half].at[:, pl.ds(col, HEAD_WIDTH)], outs[at].at[half])
            at += 1
    for first, count in chunks:
        for x in range(lay.group):
            col = pl.multiple_of(
                (lay.column(x, u) * GROUP_WIDTH + first) * HEAD_WIDTH, HEAD_WIDTH
            )
            for half in range(2):
                add(ins[half].at[:, pl.ds(col, count * HEAD_WIDTH)], outs[at].at[half])
            at += 1
    run_copies(copies)


def pack(lay, u, chunks, queries, cotangent, kv=()):
    ins = (queries, cotangent) + tuple(kv)
    shapes = []
    if kv:
        shapes += [(2, lay.tokens, HEAD_WIDTH)] * lay.group
    for _, count in chunks:
        shapes += [(2, lay.tokens, count * HEAD_WIDTH)] * lay.group
    moved = 2 * sum(2 * math.prod(s) for s in shapes)
    outs = pl.pallas_call(
        functools.partial(pack_kernel, lay, chunks, bool(kv)),
        out_shape=[jax.ShapeDtypeStruct(s, jnp.bfloat16) for s in shapes],
        in_specs=[pl.BlockSpec(memory_space=pltpu.SMEM)]
        + [pl.BlockSpec(memory_space=pltpu.VMEM)] * len(ins),
        out_specs=[pl.BlockSpec(memory_space=pl.ANY)] * len(shapes),
        scratch_shapes=[pltpu.SemaphoreType.DMA((2 * len(shapes),))],
        compiler_params=pltpu.CompilerParams(vmem_limit_bytes=VMEM_BYTES),
        cost_estimate=pl.CostEstimate(flops=0, transcendentals=0, bytes_accessed=moved),
        name="pack",
    )(u, *ins)
    return [outs[i : i + lay.group] for i in range(0, len(outs), lay.group)]


def collect_kernel(lay, *refs):
    slabs, (k_ref, v_ref, sems) = refs[: lay.group], refs[lay.group :]
    copies = []
    for x in range(lay.group):
        rows = pl.ds(x * lay.tokens, lay.tokens)
        for half, dst in enumerate((k_ref, v_ref)):
            copies.append(
                pltpu.make_async_copy(slabs[x].at[half], dst.at[rows], sems.at[len(copies)])
            )
    run_copies(copies)


def collect(lay, slabs):
    shape = jax.ShapeDtypeStruct((lay.table, HEAD_WIDTH), jnp.bfloat16)
    return pl.pallas_call(
        functools.partial(collect_kernel, lay),
        out_shape=[shape, shape],
        in_specs=[pl.BlockSpec(memory_space=pl.ANY)] * lay.group,
        out_specs=[pl.BlockSpec(memory_space=pltpu.VMEM)] * 2,
        scratch_shapes=[pltpu.SemaphoreType.DMA((2 * lay.group,))],
        cost_estimate=pl.CostEstimate(
            flops=0, transcendentals=0, bytes_accessed=8 * lay.table * HEAD_WIDTH
        ),
        name="collect",
    )(*slabs)


def attention_kernel(lay, heads, first, last, list_ref, count_ref, *refs):
    refs = list(refs)

    def take(n):
        taken = refs[:n]
        del refs[:n]
        return taken

    slabs, keys, values = take(lay.group), take(lay.areas), take(lay.areas)
    sums_in = [] if first else take(2)
    outs = take(lay.group)
    if last:
        dk_out, dv_out = take(lay.areas), take(lay.areas)
    else:
        sums_out = take(2)
    (q_scr, do_scr, o_scr, gq_scr, k_tab, v_tab, dk_acc, dv_acc) = take(8)
    (s_scr, e_scr, m_scr, o_acc, gq_acc, sems) = take(6)
    if last:
        dk_narrow, dv_narrow = take(2)
    area = lay.own_blocks
    copies, late = [], []

    def add(where, src, dst):
        n = len(copies) + len(late)
        where.append(pltpu.make_async_copy(src, dst, sems.at[n]))

    def place(x):
        block, row = divmod(x * lay.tokens, BLOCK_TOKENS)
        return block, pl.ds(row, lay.tokens)

    for x in range(lay.group):
        block, rows = place(x)
        add(copies, slabs[x].at[0], q_scr.at[block, rows])
        add(copies, slabs[x].at[1], do_scr.at[block, rows])
    for a in range(lay.areas):
        add(copies, keys[a], k_tab.at[pl.ds(a * area, area)])
        add(copies, values[a], v_tab.at[pl.ds(a * area, area)])
    if not first:
        add(late, sums_in[0], dk_acc)
        add(late, sums_in[1], dv_acc)
    for copy in copies + late:
        copy.start()
    if first:
        dk_acc[...] = jnp.zeros_like(dk_acc)
        dv_acc[...] = jnp.zeros_like(dv_acc)
    for copy in copies + late:
        copy.wait()

    repeat = BLOCK_TOKENS // HEAD_WIDTH

    def widen(x):
        return jnp.concatenate([x] * repeat, axis=1)

    def one(t, carry):
        v, j = t // heads, t % heads
        live = count_ref[v]
        cols = pl.ds(pl.multiple_of(j * HEAD_WIDTH, HEAD_WIDTH), HEAD_WIDTH)

        m_scr[...] = jnp.full_like(m_scr, LOWEST)

        def scores(i, c):
            block = list_ref[v, i]
            s = dot(q_scr[v, :, cols], k_tab[block], NT)
            s_scr[i] = s
            m = m_scr[...]
            for part in range(repeat):
                m = jnp.maximum(m, s[:, part * HEAD_WIDTH : (part + 1) * HEAD_WIDTH])
            m_scr[...] = m
            return c

        lax.fori_loop(0, live, scores, 0)
        top = jnp.max(m_scr[...], axis=1, keepdims=True)
        m_scr[...] = jnp.broadcast_to(top, m_scr.shape)
        o_acc[...] = jnp.zeros_like(o_acc)

        def weigh(i, c):
            block = list_ref[v, i]
            e = jnp.exp2((s_scr[i] - widen(m_scr[...])) * EXP2_SCALE).astype(jnp.bfloat16)
            e_scr[i] = e
            ones = jnp.ones((BLOCK_TOKENS, HEAD_WIDTH), jnp.bfloat16)
            o_acc[...] += dot(e, jnp.concatenate([v_tab[block], ones], axis=1), NN)
            return c

        lax.fori_loop(0, live, weigh, 0)
        inverse = 1.0 / o_acc[:, HEAD_WIDTH:]
        attended = (o_acc[:, :HEAD_WIDTH] * inverse).astype(jnp.bfloat16)
        o_scr[v, :, cols] = attended
        cot = do_scr[v, :, cols].astype(jnp.float32)
        delta = jnp.sum(attended.astype(jnp.float32) * cot, axis=1, keepdims=True)
        m_scr[...] = delta * inverse
        do_scr[v, :, cols] = (cot * inverse).astype(jnp.bfloat16)
        gq_acc[...] = jnp.zeros_like(gq_acc)

        def grads(i, c):
            block = list_ref[v, i]
            cot_n = do_scr[v, :, cols]
            e = e_scr[i]
            dp = dot(cot_n, v_tab[block], NT)
            ds = e * (dp - widen(m_scr[...])).astype(jnp.bfloat16)
            gq_acc[...] += dot(ds, k_tab[block], NN)
            dk_acc[block] += dot(ds, q_scr[v, :, cols], TN)
            dv_acc[block] += dot(e, cot_n, TN)
            return c

        lax.fori_loop(0, live, grads, 0)
        gq_scr[v, :, cols] = (gq_acc[...] * SCORE_SCALE).astype(jnp.bfloat16)
        return carry

    lax.fori_loop(0, lay.own_blocks * heads, one, 0)

    copies = []
    for x in range(lay.group):
        block, rows = place(x)
        add(copies, o_scr.at[block, rows], outs[x].at[0])
        add(copies, gq_scr.at[block, rows], outs[x].at[1])
    late = []
    if last:
        for b in range(lay.blocks):
            dk_narrow[b] = (dk_acc[b] * SCORE_SCALE).astype(jnp.bfloat16)
            dv_narrow[b] = dv_acc[b].astype(jnp.bfloat16)
        for a in range(lay.areas):
            add(copies, dk_narrow.at[pl.ds(a * area, area)], dk_out[a])
            add(copies, dv_narrow.at[pl.ds(a * area, area)], dv_out[a])
    else:
        add(copies, dk_acc, sums_out[0])
        add(copies, dv_acc, sums_out[1])
    run_copies(copies)


def attention(lay, heads, first, last, lists, counts, slabs, keys, values, sums):
    bf, f32 = jnp.bfloat16, jnp.float32
    width = heads * HEAD_WIDTH
    area = (lay.own_blocks, BLOCK_TOKENS, HEAD_WIDTH)
    whole = (lay.blocks, BLOCK_TOKENS, HEAD_WIDTH)
    out_shape = [jax.ShapeDtypeStruct((2, lay.tokens, width), bf)] * lay.group
    if last:
        out_shape += [jax.ShapeDtypeStruct(area, bf)] * (2 * lay.areas)
    else:
        out_shape += [jax.ShapeDtypeStruct(whole, f32)] * 2
    most = lists.shape[1]
    tile = (BLOCK_TOKENS, HEAD_WIDTH)
    scratch = [pltpu.VMEM((lay.own_blocks, BLOCK_TOKENS, width), bf)] * 4
    scratch += [pltpu.VMEM(whole, bf)] * 2 + [pltpu.VMEM(whole, f32)] * 2
    scratch += [
        pltpu.VMEM((most, BLOCK_TOKENS, BLOCK_TOKENS), f32),
        pltpu.VMEM((most, BLOCK_TOKENS, BLOCK_TOKENS), bf),
        pltpu.VMEM(tile, f32),
        pltpu.VMEM((BLOCK_TOKENS, 2 * HEAD_WIDTH), f32),
        pltpu.VMEM(tile, f32),
        pltpu.SemaphoreType.DMA((2 * lay.group + 2 * lay.areas + 2,)),
    ]
    if last:
        scratch += [pltpu.VMEM(whole, bf)] * 2
    keys = [k.reshape(area) for k in keys]
    values = [v.reshape(area) for v in values]
    operands = [*slabs, *keys, *values, *sums]
    tiles = lay.own_blocks * heads * most // 2
    return pl.pallas_call(
        functools.partial(attention_kernel, lay, heads, first, last),
        out_shape=out_shape,
        grid_spec=pltpu.PrefetchScalarGridSpec(
            num_scalar_prefetch=2,
            grid=(1,),
            in_specs=[pl.BlockSpec(memory_space=pl.ANY)] * len(operands),
            out_specs=[pl.BlockSpec(memory_space=pl.ANY)] * len(out_shape),
            scratch_shapes=scratch,
        ),
        compiler_params=pltpu.CompilerParams(vmem_limit_bytes=VMEM_BYTES),
        cost_estimate=pl.CostEstimate(
            flops=tiles * 12 * BLOCK_TOKENS * BLOCK_TOKENS * HEAD_WIDTH * 2,
            transcendentals=tiles * BLOCK_TOKENS * BLOCK_TOKENS,
            bytes_accessed=16 * 1024 * 1024,
        ),
        name="attention",
    )(lists, counts, *operands)


def split_kernel(lay, *refs):
    (k0, k1, v0, v1), outs = refs[:4], refs[4:]
    for x in range(lay.group):
        rows = pl.ds(x * lay.tokens, lay.tokens)
        for half, (a, b) in enumerate(((k0, k1), (v0, v1))):
            total = a[rows].astype(jnp.float32) + b[rows].astype(jnp.float32)
            outs[x][half] = total.astype(jnp.bfloat16)


def split(lay, k0, k1, v0, v1):
    shape = jax.ShapeDtypeStruct((2, lay.tokens, HEAD_WIDTH), jnp.bfloat16)
    return pl.pallas_call(
        functools.partial(split_kernel, lay),
        out_shape=[shape] * lay.group,
        in_specs=[pl.BlockSpec(memory_space=pltpu.VMEM)] * 4,
        out_specs=[pl.BlockSpec(memory_space=pltpu.VMEM)] * lay.group,
        cost_estimate=pl.CostEstimate(
            flops=0, transcendentals=0, bytes_accessed=12 * lay.table * HEAD_WIDTH
        ),
        name="split",
    )(k0, k1, v0, v1)


def unpack_kernel(lay, chunks, u_ref, *refs):
    n_in = lay.group * (len(chunks) + 1)
    ins, refs = refs[:n_in], refs[n_in:]
    outs, sems = refs[:4], refs[4]
    u = u_ref[0]
    copies = []

    def add(src, dst):
        copies.append(pltpu.make_async_copy(src, dst, sems.at[len(copies)]))

    at = 0
    for first, count in chunks:
        for x in range(lay.group):
            col = pl.multiple_of(
                (lay.column(x, u) * GROUP_WIDTH + first) * HEAD_WIDTH, HEAD_WIDTH
            )
            for half in range(2):
                add(ins[at].at[half], outs[half].at[:, pl.ds(col, count * HEAD_WIDTH)])
            at += 1
    for x in range(lay.group):
        col = pl.multiple_of(lay.column(x, u) * HEAD_WIDTH, HEAD_WIDTH)
        for half in range(2):
            add(ins[at].at[half], outs[2 + half].at[:, pl.ds(col, HEAD_WIDTH)])
        at += 1
    run_copies(copies)


def unpack(lay, u, chunks, slabs, kv_slabs):
    ins = [s for chunk in slabs for s in chunk] + list(kv_slabs)
    bf = jnp.bfloat16
    wide = jax.ShapeDtypeStruct((lay.tokens, QUERY_HEADS * HEAD_WIDTH), bf)
    narrow = jax.ShapeDtypeStruct((lay.tokens, KEY_VALUE_HEADS * HEAD_WIDTH), bf)
    out_shape = [wide, wide, narrow, narrow]
    moved = 4 * sum(math.prod(s.shape) for s in out_shape)
    return pl.pallas_call(
        functools.partial(unpack_kernel, lay, chunks),
        out_shape=out_shape,
        in_specs=[pl.BlockSpec(memory_space=pltpu.SMEM)]
        + [pl.BlockSpec(memory_space=pl.ANY)] * len(ins),
        out_specs=[pl.BlockSpec(memory_space=pltpu.VMEM)] * 4,
        scratch_shapes=[pltpu.SemaphoreType.DMA((2 * len(ins),))],
        compiler_params=pltpu.CompilerParams(vmem_limit_bytes=VMEM_BYTES),
        cost_estimate=pl.CostEstimate(flops=0, transcendentals=0, bytes_accessed=moved),
        name="unpack",
    )(u, *ins)


def gather_areas(lay, own, bits):
    tables = {0: own}
    for bit in bits:
        for p in sorted(tables):
            tables[p | bit] = lay.permute(tables[p], xa=bit)
    return [tables[p] for p in range(lay.areas)]


def reduce_areas(lay, parts, bits):
    parts = dict(enumerate(parts))
    for bit in bits[:-1]:
        for p in sorted(parts):
            if p & bit:
                other = lay.permute(parts.pop(p), xa=bit)
                total = parts[p ^ bit].astype(jnp.float32) + other.astype(jnp.float32)
                parts[p ^ bit] = total.astype(jnp.bfloat16)
    return parts[0], lay.permute(parts[bits[-1]], xa=bits[-1])


def shards(ctx_size, head_size, queries, keys, values, cotangent, block_list, block_count):
    lay = Layout(ctx_size, head_size, queries.shape[0])
    ctx_rank, head_rank = lax.axis_index("ctx"), lax.axis_index("head")
    u = head_rank * lay.subs + lax.rem(ctx_rank, lay.subs)
    u = jnp.reshape(u, (1,)).astype(jnp.int32)
    base = ctx_rank * lay.blocks_per_ctx + head_rank // (BLOCK_TOKENS // lay.tokens)
    base = base.astype(jnp.int32)
    own_rows = jnp.bitwise_xor(jnp.arange(lay.own_blocks, dtype=jnp.int32), base)
    lists = jnp.bitwise_xor(jnp.take(block_list, own_rows, axis=0), base)
    counts = jnp.take(block_count, own_rows, axis=0)

    chunks, at = [], 0
    for count in CHUNKS:
        chunks.append((at, count))
        at += count
    kv_out, *first_out = pack(lay, u, chunks[:1], queries, cotangent, (keys, values))
    kv_in = lay.exchange(kv_out)
    rest_out = pack(lay, u, chunks[1:], queries, cotangent) if len(chunks) > 1 else []
    own_k, own_v = collect(lay, kv_in)
    bits = [1 << i for i in range(lay.areas.bit_length() - 1)]
    key_tables = gather_areas(lay, own_k, bits)
    value_tables = gather_areas(lay, own_v, bits[::-1])

    slabs = [lay.exchange(s) for s in first_out + rest_out]
    sums, results = [], []
    for n, (_, count) in enumerate(chunks):
        last = n == len(chunks) - 1
        outs = attention(
            lay, count, n == 0, last, lists, counts, slabs[n], key_tables, value_tables, sums
        )
        sums = outs[lay.group :]
        results.append(lay.exchange(outs[: lay.group]))
    flat = [s.reshape(lay.table, HEAD_WIDTH) for s in sums]
    k0, k1 = reduce_areas(lay, flat[: lay.areas], bits[::-1])
    v0, v1 = reduce_areas(lay, flat[lay.areas :], bits)
    kv_grads = lay.exchange(split(lay, k0, k1, v0, v1))
    return tuple(unpack(lay, u, chunks, results, kv_grads))


def solution(mesh):
    placed = P(("ctx", "head"), None)
    return jax.shard_map(
        functools.partial(shards, mesh.shape["ctx"], mesh.shape["head"]),
        mesh=mesh,
        in_specs=(placed,) * 4 + (P(), P()),
        out_specs=(placed,) * 4,
        check_vma=False,
    )
```

```python
import functools
import math

import jax
import jax.numpy as jnp
from jax import lax
from jax.experimental import pallas as pl
from jax.experimental.pallas import tpu as pltpu
from jax.sharding import PartitionSpec as P


QUERY_HEADS = 48
KEY_VALUE_HEADS = 8
HEAD_WIDTH = 128
BLOCK_TOKENS = 512
GROUP_WIDTH = QUERY_HEADS // KEY_VALUE_HEADS

SCORE_SCALE = HEAD_WIDTH ** (-0.5)
EXP2_SCALE = SCORE_SCALE * math.log2(math.e)
LOWEST = -3.0e38
VMEM_BYTES = 62 * 1024 * 1024


NT = (((1,), (1,)), ((), ()))
NN = (((1,), (0,)), ((), ()))
TN = (((0,), (0,)), ((), ()))


def dot(a, b, dims):
    return lax.dot_general(a, b, dims, preferred_element_type=jnp.float32)


def bf16(*shape):
    return jax.ShapeDtypeStruct(shape, jnp.bfloat16)


ANY = pl.BlockSpec(memory_space=pl.ANY)
VMEM = pl.BlockSpec(memory_space=pltpu.VMEM)
SMEM = pl.BlockSpec(memory_space=pltpu.SMEM)


class Copies:
    def __init__(self, sems):
        self.sems, self.made = sems, 0

    def make(self, src, dst):
        self.made += 1
        return pltpu.make_async_copy(src, dst, self.sems.at[self.made - 1])

    @staticmethod
    def run(copies):
        for copy in copies:
            copy.start()
        for copy in copies:
            copy.wait()


class Layout:
    def __init__(self, ctx_size, head_size, tokens):
        self.group = KEY_VALUE_HEADS
        assert ctx_size % self.group == 0
        self.ctx_size, self.heads, self.tokens = ctx_size, head_size, tokens
        self.line = ctx_size // self.group * head_size
        self.per_ctx = tokens * head_size // BLOCK_TOKENS
        self.per_block = BLOCK_TOKENS // tokens
        self.blocks = ctx_size * self.per_ctx
        self.others = range(1, self.group)

    def device(self, w, u):
        m, h = divmod(w, self.heads)
        return (m * self.group + u) * self.heads + h

    def swap(self, value, x):
        pairs = [
            (self.device(w, u), self.device(w, u ^ x))
            for w in range(self.line)
            for u in range(self.group)
        ]
        return lax.ppermute(value, ("ctx", "head"), pairs)

    def shift(self, value, sources, step):
        pairs = [
            (self.device(w, u), self.device(w + step, u)) for w in sources for u in range(self.group)
        ]
        return lax.ppermute(value, ("ctx", "head"), pairs)

    def place(self, w):
        m, h = w // self.heads, w % self.heads
        first = (m * self.per_ctx + h // self.per_block) * self.group
        return first, pl.multiple_of(h % self.per_block * self.tokens, self.tokens)

    def table_block(self, block, u):
        ctx = block // self.per_ctx
        first = (ctx // self.group * self.per_ctx + block % self.per_ctx) * self.group
        return first + jnp.bitwise_xor(ctx % self.group, u)


def copy_call(body, ins, specs, outs, n, out_spec=ANY):
    def kernel(*refs):
        sems = refs[-1]
        Copies.run(list(body(Copies(sems), refs[: len(ins)], refs[len(ins) : -1])))

    moved = 4 * sum(math.prod(o.shape) for o in outs)
    return pl.pallas_call(
        kernel,
        out_shape=outs,
        in_specs=specs,
        out_specs=[out_spec] * len(outs),
        scratch_shapes=[pltpu.SemaphoreType.DMA((n,))],
        compiler_params=pltpu.CompilerParams(vmem_limit_bytes=VMEM_BYTES),
        cost_estimate=pl.CostEstimate(flops=0, transcendentals=0, bytes_accessed=moved),
    )(*ins)


def columns(index, count=1):
    return pl.ds(pl.multiple_of(index * HEAD_WIDTH, HEAD_WIDTH), count * HEAD_WIDTH)


def pack(lay, u, arrays, count, places):
    def body(copies, ins, outs):
        rank, *raw = ins
        for x, out in zip(places, outs, strict=True):
            cols = columns(jnp.bitwise_xor(rank[0], x) * count, count)
            for half in range(2):
                yield copies.make(raw[half].at[:, cols], out.at[half])

    outs = [bf16(2, lay.tokens, count * HEAD_WIDTH)] * len(places)
    return copy_call(body, [u, *arrays], [SMEM, VMEM, VMEM], outs, 2 * len(places))


def unpack(lay, u, slabs, count):
    def body(copies, ins, outs):
        rank, *parts = ins
        for x, part in enumerate(parts):
            cols = columns(jnp.bitwise_xor(rank[0], x) * count, count)
            for half in range(2):
                yield copies.make(part.at[half], outs[half].at[:, cols])

    outs = [bf16(lay.tokens, lay.group * count * HEAD_WIDTH)] * 2
    specs = [SMEM] + [ANY] * lay.group
    return copy_call(body, [u, *slabs], specs, outs, 2 * lay.group, VMEM)


def collect(lay, slabs):
    def body(copies, ins, outs):
        for x, part in enumerate(ins):
            for half in range(2):
                yield copies.make(part.at[half], outs[0].at[half, x])

    outs = [bf16(2, lay.group, lay.tokens, HEAD_WIDTH)]
    specs = [ANY] * lay.group
    return copy_call(body, list(slabs), specs, outs, 2 * lay.group, VMEM)[0]


def split(lay, terms):
    def kernel(*refs):
        ins, outs = refs[: len(terms)], refs[len(terms) :]
        for x, out in enumerate(outs):
            for half in range(2):
                total = ins[0][half, x].astype(jnp.float32)
                for term in ins[1:]:
                    total += term[half, x].astype(jnp.float32)
                out[half] = total.astype(jnp.bfloat16)

    outs = [bf16(2, lay.tokens, HEAD_WIDTH)] * lay.group
    moved = 2 * (len(terms) + 1) * math.prod(terms[0].shape)
    return pl.pallas_call(
        kernel,
        out_shape=outs,
        in_specs=[VMEM] * len(terms),
        out_specs=[VMEM] * len(outs),
        cost_estimate=pl.CostEstimate(flops=0, transcendentals=0, bytes_accessed=moved),
        name="split",
    )(*terms)


def attention_kernel(lay, list_ref, count_ref, where_ref, *refs):
    refs = list(refs)

    def take(n):
        taken = refs[:n]
        del refs[:n]
        return taken

    raw, slabs = take(2), take(lay.group - 1)
    own_table, below, above = take(1)[0], take(lay.line - 1), take(lay.line - 1)
    outs, own_sums, to_below, to_above = take(lay.group), take(1)[0], take(lay.line - 1), take(lay.line - 1)
    q_scr, do_scr, k_tab, v_tab, dk_acc, dv_acc, s_scr, e_scr, m_scr, o_acc, gq_acc, o_scr, sems = refs
    u, w = where_ref[0], where_ref[1]
    heads, rows = GROUP_WIDTH, lay.tokens
    made = Copies(sems)

    def table_copies(plane, table):
        first, row = lay.place(plane)
        dst = pl.ds(first, lay.group), pl.ds(row, rows)
        return [made.make(table.at[0], k_tab.at[dst]), made.make(table.at[1], v_tab.at[dst])]

    copies = []
    for x in range(lay.group):
        for half, dst in enumerate((q_scr, do_scr)):
            if x == 0:
                src = raw[half].at[:, columns(u * heads, heads)]
            else:
                src = slabs[x - 1].at[half]
            copies.append(made.make(src, dst.at[x]))
    copies += table_copies(w, own_table)
    guarded = []
    for k in range(1, lay.line):
        guarded.append((w >= k, table_copies(w - k, below[k - 1])))
        guarded.append((w + k < lay.line, table_copies(w + k, above[k - 1])))
    for copy in copies:
        copy.start()
    for valid, some in guarded:

        @pl.when(valid)
        def _():
            for copy in some:
                copy.start()

    dk_acc[...] = jnp.zeros_like(dk_acc)
    dv_acc[...] = jnp.zeros_like(dv_acc)
    for copy in copies:
        copy.wait()
    for valid, some in guarded:

        @pl.when(valid)
        def _():
            for copy in some:
                copy.wait()

    repeat = BLOCK_TOKENS // HEAD_WIDTH

    def widen(x):
        return jnp.concatenate([x] * repeat, axis=1)

    cols = [pl.ds(g * HEAD_WIDTH, HEAD_WIDTH) for g in range(heads)]
    results = [
        [made.make(src.at[x], outs[x].at[half]) for half, src in enumerate((do_scr, q_scr))]
        for x in range(lay.group)
    ]
    plane_block = w // lay.heads * lay.group * lay.per_ctx + w % lay.heads // lay.per_block

    def one(x, carry):
        mine = plane_block + jnp.bitwise_xor(u, x) * lay.per_ctx
        live = count_ref[mine]
        m_scr[...] = jnp.full_like(m_scr, LOWEST)

        def scores(i, c):
            block = lay.table_block(list_ref[mine, i], u)
            for g in range(heads):
                s = dot(q_scr[x, :, cols[g]], k_tab[block], NT)
                s_scr[i, g] = s
                m = m_scr[g]
                for part in range(repeat):
                    m = jnp.maximum(m, s[:, part * HEAD_WIDTH : (part + 1) * HEAD_WIDTH])
                m_scr[g] = m
            return c

        lax.fori_loop(0, live, scores, 0)
        for g in range(heads):
            top = jnp.max(m_scr[g], axis=1, keepdims=True)
            m_scr[g] = jnp.broadcast_to(top, m_scr.shape[1:])
        o_acc[...] = jnp.zeros_like(o_acc)

        def weigh(i, c):
            block = lay.table_block(list_ref[mine, i], u)
            ones = jnp.ones((BLOCK_TOKENS, HEAD_WIDTH), jnp.bfloat16)
            v_ones = jnp.concatenate([v_tab[block], ones], axis=1)
            for g in range(heads):
                e = jnp.exp2((s_scr[i, g] - widen(m_scr[g])) * EXP2_SCALE)
                e = e.astype(jnp.bfloat16)
                e_scr[i, g] = e
                o_acc[g] += dot(e, v_ones, NN)
            return c

        lax.fori_loop(0, live, weigh, 0)
        for g in range(heads):
            inverse = 1.0 / o_acc[g, :, HEAD_WIDTH:]
            attended = (o_acc[g, :, :HEAD_WIDTH] * inverse).astype(jnp.bfloat16)
            o_scr[:, cols[g]] = attended
            cot = do_scr[x, :, cols[g]].astype(jnp.float32)
            delta = jnp.sum(attended.astype(jnp.float32) * cot, axis=1, keepdims=True)
            m_scr[g] = delta * inverse
            do_scr[x, :, cols[g]] = (cot * inverse).astype(jnp.bfloat16)
        gq_acc[...] = jnp.zeros_like(gq_acc)

        def grads(i, c):
            block = lay.table_block(list_ref[mine, i], u)
            dk, dv = None, None
            for g in range(heads):
                cot_n = do_scr[x, :, cols[g]]
                e = e_scr[i, g]
                dp = dot(cot_n, v_tab[block], NT)
                ds = e * (dp - widen(m_scr[g])).astype(jnp.bfloat16)
                gq_acc[g] += dot(ds, k_tab[block], NN)
                dk_g = dot(ds, q_scr[x, :, cols[g]], TN)
                dv_g = dot(e, cot_n, TN)
                dk = dk_g if dk is None else dk + dk_g
                dv = dv_g if dv is None else dv + dv_g
            dk_acc[block] += dk
            dv_acc[block] += dv
            return c

        lax.fori_loop(0, live, grads, 0)
        for g in range(heads):
            q_scr[x, :, cols[g]] = (gq_acc[g] * SCORE_SCALE).astype(jnp.bfloat16)
        do_scr[x] = o_scr[...]
        for place in range(lay.group):

            @pl.when(x == place)
            def _():
                for copy in results[place]:
                    copy.start()

        return carry

    lax.fori_loop(0, lay.group, one, 0)

    def narrow(b, carry):
        k_tab[b] = (dk_acc[b] * SCORE_SCALE).astype(jnp.bfloat16)
        v_tab[b] = dv_acc[b].astype(jnp.bfloat16)
        return carry

    lax.fori_loop(0, lay.blocks, narrow, 0)

    def sum_copies(plane, out):
        first, row = lay.place(plane)
        src = pl.ds(first, lay.group), pl.ds(row, rows)
        return [made.make(k_tab.at[src], out.at[0]), made.make(v_tab.at[src], out.at[1])]

    copies = sum_copies(w, own_sums)
    guarded = []
    for k in range(1, lay.line):
        guarded.append((w >= k, sum_copies(w - k, to_below[k - 1])))
        guarded.append((w + k < lay.line, sum_copies(w + k, to_above[k - 1])))
    for copy in copies:
        copy.start()
    for valid, some in guarded:

        @pl.when(valid)
        def _():
            for copy in some:
                copy.start()

    for valid, some in guarded:

        @pl.when(valid)
        def _():
            for copy in some:
                copy.wait()

    for copy in copies + [c for some in results for c in some]:
        copy.wait()


def attention(lay, lists, counts, where, raw, slabs, own_table, below, above):
    bf, f32 = jnp.bfloat16, jnp.float32
    width = GROUP_WIDTH * HEAD_WIDTH
    whole = (lay.blocks, BLOCK_TOKENS, HEAD_WIDTH)
    own = (lay.group, lay.tokens, width)
    most = lists.shape[1]
    tile = (GROUP_WIDTH, lay.tokens, BLOCK_TOKENS)
    far = 2 * (lay.line - 1)
    scratch = [
        *[pltpu.VMEM(own, bf)] * 2,
        *[pltpu.VMEM(whole, bf)] * 2,
        *[pltpu.VMEM(whole, f32)] * 2,
        pltpu.VMEM((most, *tile), f32),
        pltpu.VMEM((most, *tile), bf),
        pltpu.VMEM((GROUP_WIDTH, lay.tokens, HEAD_WIDTH), f32),
        pltpu.VMEM((GROUP_WIDTH, lay.tokens, 2 * HEAD_WIDTH), f32),
        pltpu.VMEM((GROUP_WIDTH, lay.tokens, HEAD_WIDTH), f32),
        pltpu.VMEM((lay.tokens, width), bf),
        pltpu.SemaphoreType.DMA((4 * lay.group + 4 * far + 4,)),
    ]
    table = (2, lay.group, lay.tokens, HEAD_WIDTH)
    out_shape = [bf16(2, lay.tokens, width)] * lay.group + [bf16(*table)] * (1 + far)
    operands = [*raw, *slabs, own_table, *below, *above]
    tiles = lay.group * most // 2
    return pl.pallas_call(
        functools.partial(attention_kernel, lay),
        out_shape=out_shape,
        grid_spec=pltpu.PrefetchScalarGridSpec(
            num_scalar_prefetch=3,
            grid=(1,),
            in_specs=[ANY] * len(operands),
            out_specs=[ANY] * len(out_shape),
            scratch_shapes=scratch,
        ),
        compiler_params=pltpu.CompilerParams(vmem_limit_bytes=VMEM_BYTES),
        cost_estimate=pl.CostEstimate(
            flops=tiles * 24 * math.prod(tile) * HEAD_WIDTH,
            transcendentals=tiles * math.prod(tile),
            bytes_accessed=32 * 1024 * 1024,
        ),
        name="attention",
    )(lists, counts, where, *operands)


def add(a, b):
    return (a.astype(jnp.float32) + b.astype(jnp.float32)).astype(jnp.bfloat16)


def shards(ctx_size, head_size, queries, keys, values, cotangent, block_list, block_count):
    lay = Layout(ctx_size, head_size, queries.shape[0])
    ctx_rank, head_rank = lax.axis_index("ctx"), lax.axis_index("head")
    u = lax.rem(ctx_rank, lay.group)
    w = ctx_rank // lay.group * lay.heads + head_rank
    where = jnp.stack([u, w]).astype(jnp.int32)
    n = lay.line

    local, *sent = pack(lay, where, (keys, values), 1, range(lay.group))
    came = [lay.swap(s, x) for x, s in zip(lay.others, sent)]
    own_table = collect(lay, [local, *came])
    below, above = [own_table], [own_table]
    for k in range(1, n):
        below.append(lay.shift(below[-1], range(k - 1, n - 1), 1))
        above.append(lay.shift(above[-1], range(1, n - k + 1), -1))
    sent = pack(lay, where, (queries, cotangent), GROUP_WIDTH, lay.others)
    slabs = [lay.swap(s, x) for x, s in zip(lay.others, sent)]
    outs = attention(
        lay,
        block_list,
        block_count,
        where,
        (queries, cotangent),
        slabs,
        own_table,
        below[1:],
        above[1:],
    )
    slabs, outs = outs[: lay.group], outs[lay.group :]
    own_sums, to_below, to_above = outs[0], outs[1:n], outs[n:]
    up, down = to_above[n - 2], to_below[n - 2]
    for k in range(n - 1, 0, -1):
        up = lay.shift(up, range(0, n - k), 1)
        down = lay.shift(down, range(k, n), -1)
        if k > 1:
            up, down = add(up, to_above[k - 2]), add(down, to_below[k - 2])
    local, *sent = split(lay, [own_sums, up, down])
    came = [lay.swap(s, x) for x, s in zip(lay.others, sent)]
    key_grad, value_grad = unpack(lay, where, [local, *came], 1)
    came = [lay.swap(s, x) for x, s in zip(lay.others, slabs[1:])]
    attn_out, grad_query = unpack(lay, where, [slabs[0], *came], GROUP_WIDTH)
    return attn_out, grad_query, key_grad, value_grad


def solution(mesh):
    placed = P(("ctx", "head"), None)

    def body(*args):
        return shards(mesh.shape["ctx"], mesh.shape["head"], *args)

    return jax.shard_map(
        body,
        mesh=mesh,
        in_specs=(placed,) * 4 + (P(), P()),
        out_specs=(placed,) * 4,
        check_vma=False,
    )
```

```python
import functools
import math

import jax
import jax.numpy as jnp
from jax import lax
from jax.experimental import pallas as pl
from jax.experimental.pallas import tpu as pltpu
from jax.sharding import PartitionSpec as P


QUERY_HEADS = 48
KEY_VALUE_HEADS = 8
HEAD_WIDTH = 128
BLOCK_TOKENS = 512
GROUP_WIDTH = QUERY_HEADS // KEY_VALUE_HEADS

SCORE_SCALE = HEAD_WIDTH ** (-0.5)
EXP2_SCALE = SCORE_SCALE * math.log2(math.e)
LOWEST = -3.0e38
VMEM_BYTES = 62 * 1024 * 1024


NT = (((1,), (1,)), ((), ()))
NN = (((1,), (0,)), ((), ()))
TN = (((0,), (0,)), ((), ()))


def dot(a, b, dims):
    return lax.dot_general(a, b, dims, preferred_element_type=jnp.float32)


def bf16(*shape):
    return jax.ShapeDtypeStruct(shape, jnp.bfloat16)


ANY = pl.BlockSpec(memory_space=pl.ANY)
VMEM = pl.BlockSpec(memory_space=pltpu.VMEM)
SMEM = pl.BlockSpec(memory_space=pltpu.SMEM)


class Copies:
    def __init__(self, sems):
        self.sems, self.made = sems, 0

    def make(self, src, dst):
        self.made += 1
        return pltpu.make_async_copy(src, dst, self.sems.at[self.made - 1])

    @staticmethod
    def run(copies):
        for copy in copies:
            copy.start()
        for copy in copies:
            copy.wait()


class Layout:
    def __init__(self, ctx_size, head_size, tokens):
        self.group = KEY_VALUE_HEADS
        assert ctx_size % self.group == 0
        self.ctx_size, self.heads, self.tokens = ctx_size, head_size, tokens
        self.line = ctx_size // self.group * head_size
        self.per_ctx = tokens * head_size // BLOCK_TOKENS
        self.per_block = BLOCK_TOKENS // tokens
        self.blocks = ctx_size * self.per_ctx
        self.others = range(1, self.group)

    def device(self, w, u):
        m, h = divmod(w, self.heads)
        return (m * self.group + u) * self.heads + h

    def swap(self, value, x):
        pairs = [
            (self.device(w, u), self.device(w, u ^ x))
            for w in range(self.line)
            for u in range(self.group)
        ]
        return lax.ppermute(value, ("ctx", "head"), pairs)

    def shift(self, value, sources, step):
        pairs = [
            (self.device(w, u), self.device(w + step, u)) for w in sources for u in range(self.group)
        ]
        return lax.ppermute(value, ("ctx", "head"), pairs)

    def place(self, w):
        m, h = w // self.heads, w % self.heads
        first = (m * self.per_ctx + h // self.per_block) * self.group
        return first, pl.multiple_of(h % self.per_block * self.tokens, self.tokens)

    def query_block(self, w, u):
        ctx = w // self.heads * self.group + u
        return ctx * self.per_ctx + w % self.heads // self.per_block

    def table_block(self, block, u):
        ctx = block // self.per_ctx
        first = (ctx // self.group * self.per_ctx + block % self.per_ctx) * self.group
        return first + jnp.bitwise_xor(ctx % self.group, u)


def copy_call(body, ins, specs, outs, n, out_spec=ANY):
    def kernel(*refs):
        sems = refs[-1]
        Copies.run(list(body(Copies(sems), refs[: len(ins)], refs[len(ins) : -1])))

    moved = 4 * sum(math.prod(o.shape) for o in outs)
    return pl.pallas_call(
        kernel,
        out_shape=outs,
        in_specs=specs,
        out_specs=[out_spec] * len(outs),
        scratch_shapes=[pltpu.SemaphoreType.DMA((n,))],
        compiler_params=pltpu.CompilerParams(vmem_limit_bytes=VMEM_BYTES),
        cost_estimate=pl.CostEstimate(flops=0, transcendentals=0, bytes_accessed=moved),
    )(*ins)


def columns(index, count=1):
    return pl.ds(pl.multiple_of(index * HEAD_WIDTH, HEAD_WIDTH), count * HEAD_WIDTH)


def pack(lay, u, arrays, count, places):
    def body(copies, ins, outs):
        rank, *raw = ins
        for x, out in zip(places, outs, strict=True):
            cols = columns(jnp.bitwise_xor(rank[0], x) * count, count)
            for half in range(2):
                yield copies.make(raw[half].at[:, cols], out.at[half])

    outs = [bf16(2, lay.tokens, count * HEAD_WIDTH)] * len(places)
    return copy_call(body, [u, *arrays], [SMEM, VMEM, VMEM], outs, 2 * len(places))


def pack_one(lay, u, array, count):
    def body(copies, ins, outs):
        rank, raw = ins
        for x, out in zip(lay.others, outs, strict=True):
            cols = columns(jnp.bitwise_xor(rank[0], x) * count, count)
            yield copies.make(raw.at[:, cols], out)

    outs = [bf16(lay.tokens, count * HEAD_WIDTH)] * len(lay.others)
    return copy_call(body, [u, array], [SMEM, VMEM], outs, len(outs))


def unpack(lay, u, slabs, count):
    flat, plan = [], []
    for out, some in enumerate(slabs):
        for x, part in enumerate(some):
            plan.append((out, x, len(flat)))
            flat.append(part)
    pairs = flat[0].ndim == 3

    def body(copies, ins, outs):
        rank, *parts = ins
        for out, x, at in plan:
            cols = columns(jnp.bitwise_xor(rank[0], x) * count, count)
            if pairs:
                for half in range(2):
                    yield copies.make(parts[at].at[half], outs[half].at[:, cols])
            else:
                yield copies.make(parts[at], outs[out].at[:, cols])

    outs = [bf16(lay.tokens, lay.group * count * HEAD_WIDTH)] * (2 if pairs else len(slabs))
    specs = [SMEM] + [ANY] * len(flat)
    return copy_call(body, [u, *flat], specs, outs, 2 * len(flat), VMEM)


def collect(lay, slabs):
    def body(copies, ins, outs):
        for x, part in enumerate(ins):
            for half in range(2):
                yield copies.make(part.at[half], outs[0].at[half, x])

    outs = [bf16(2, lay.group, lay.tokens, HEAD_WIDTH)]
    specs = [ANY] * lay.group
    return copy_call(body, list(slabs), specs, outs, 2 * lay.group, VMEM)[0]


def split(lay, terms):
    def kernel(*refs):
        ins, outs = refs[: len(terms)], refs[len(terms) :]
        for x, out in enumerate(outs):
            for half in range(2):
                total = ins[0][half, x].astype(jnp.float32)
                for term in ins[1:]:
                    total += term[half, x].astype(jnp.float32)
                out[half] = total.astype(jnp.bfloat16)

    outs = [bf16(2, lay.tokens, HEAD_WIDTH)] * lay.group
    moved = 2 * (len(terms) + 1) * math.prod(terms[0].shape)
    return pl.pallas_call(
        kernel,
        out_shape=outs,
        in_specs=[VMEM] * len(terms),
        out_specs=[VMEM] * len(outs),
        cost_estimate=pl.CostEstimate(flops=0, transcendentals=0, bytes_accessed=moved),
        name="split",
    )(*terms)


def wait_all(copies):
    for copy in copies:
        copy.wait()


def start_all(copies):
    for copy in copies:
        copy.start()


def start_guarded(guarded, run=start_all):
    for valid, some in guarded:

        @pl.when(valid)
        def _():
            run(some)


def at_place(x, lists, run):
    for place, some in lists.items():

        @pl.when(x == place)
        def _():
            run(some)


REPEAT = BLOCK_TOKENS // HEAD_WIDTH
COLS = [pl.ds(g * HEAD_WIDTH, HEAD_WIDTH) for g in range(GROUP_WIDTH)]


def widen(x):
    return jnp.concatenate([x] * REPEAT, axis=1)


def score_weights(s, top):
    return jnp.exp2((s - widen(top)) * EXP2_SCALE).astype(jnp.bfloat16)


def score_grads(e, cot, v, delta):
    return e * (dot(cot, v, NT) - widen(delta)).astype(jnp.bfloat16)


def table_copies(lay, made, plane, refs, table, into, base=0):
    first, row = lay.place(plane)
    part = pl.ds(first - base, lay.group), pl.ds(row, lay.tokens)
    if into:
        return [made.make(table.at[n], ref.at[part]) for n, ref in enumerate(refs)]
    return [made.make(ref.at[part], table.at[n]) for n, ref in enumerate(refs)]


def offsets(lay, w, below, above):
    for k in range(1, len(below) + 1):
        yield w >= k, w - k, below[k - 1]
        yield w + k < lay.line, w + k, above[k - 1]


def near_tables(lay, made, w, refs, own_table, below, above):
    first = lay.place(w)[0]
    guarded = []
    for valid, plane, table in offsets(lay, w, below, above):
        valid = valid & (lay.place(plane)[0] == first)
        guarded.append((valid, table_copies(lay, made, plane, refs, table, True, first)))
    return table_copies(lay, made, w, refs, own_table, True, first), guarded


def lane_max(m, s):
    for part in range(REPEAT):
        m = jnp.maximum(m, s[:, part * HEAD_WIDTH : (part + 1) * HEAD_WIDTH])
    return m


def values_and_ones(v):
    return jnp.concatenate([v, jnp.ones((BLOCK_TOKENS, HEAD_WIDTH), jnp.bfloat16)], axis=1)


def spread(column, shape):
    return jnp.broadcast_to(column, shape)


def near_forward_kernel(lay, list_ref, count_ref, where_ref, *refs):
    refs = list(refs)

    def take(n):
        taken = refs[:n]
        del refs[:n]
        return taken

    near = lay.per_block - 1
    raw, slabs = take(1)[0], take(lay.group - 1)
    own_table, below, above = take(1)[0], take(near), take(near)
    o_out, stat_out = take(2)
    q_scr, k_tab, v_tab, s_scr, m_scr, o_acc, o_scr, st_scr, sems = refs
    u, w = where_ref[0], where_ref[1]
    heads = GROUP_WIDTH
    made = Copies(sems)
    first = lay.place(w)[0]
    copies, guarded = near_tables(lay, made, w, (k_tab, v_tab), own_table, below, above)
    loads = {}
    for x in range(lay.group):
        src = slabs[x - 1] if x else raw.at[:, columns(u * heads, heads)]
        loads[x] = [made.make(src, q_scr.at[x])]
    start_all(copies)
    start_guarded(guarded)
    for some in loads.values():
        start_all(some)
    wait_all(copies)
    start_guarded(guarded, wait_all)
    shape = (lay.tokens, HEAD_WIDTH)
    lane = lax.broadcasted_iota(jnp.int32, shape, 1)
    saves = {
        x: [made.make(o_scr.at[x % 2], o_out.at[x]), made.make(st_scr.at[x], stat_out.at[x])]
        for x in range(lay.group)
    }

    def one(x, carry):
        at_place(x, loads, wait_all)
        at_place(x, {p + 2: some for p, some in saves.items()}, lambda c: wait_all(c[:1]))
        mine = lay.query_block(w, jnp.bitwise_xor(u, x))
        live = count_ref[mine]
        m_scr[...] = jnp.full_like(m_scr, LOWEST)

        def scores(i, c):
            block = lay.table_block(list_ref[mine, i], u) - first

            @pl.when((block >= 0) & (block < lay.group))
            def _():
                for g in range(heads):
                    s = dot(q_scr[x, :, COLS[g]], k_tab[block], NT)
                    s_scr[i, g] = s
                    m_scr[g] = lane_max(m_scr[g], s)

            return c

        lax.fori_loop(0, live, scores, 0)
        stats = jnp.zeros(shape, jnp.float32)
        for g in range(heads):
            top = spread(jnp.max(m_scr[g], axis=1, keepdims=True), shape)
            m_scr[g] = top
            stats = jnp.where(lane == g, top, stats)
        o_acc[...] = jnp.zeros_like(o_acc)

        def weigh(i, c):
            block = lay.table_block(list_ref[mine, i], u) - first

            @pl.when((block >= 0) & (block < lay.group))
            def _():
                v_ones = values_and_ones(v_tab[block])
                for g in range(heads):
                    o_acc[g] += dot(score_weights(s_scr[i, g], m_scr[g]), v_ones, NN)

            return c

        lax.fori_loop(0, live, weigh, 0)
        for g in range(heads):
            o_scr[x % 2, :, COLS[g]] = o_acc[g, :, :HEAD_WIDTH]
            stats = jnp.where(lane == heads + g, o_acc[g, :, HEAD_WIDTH:], stats)
        st_scr[x] = stats
        at_place(x, saves, start_all)
        return carry

    lax.fori_loop(0, lay.group, one, 0)
    for x, some in saves.items():
        wait_all(some if x >= lay.group - 2 else some[1:])


def forward_kernel(lay, list_ref, count_ref, where_ref, *refs):
    refs = list(refs)

    def take(n):
        taken = refs[:n]
        del refs[:n]
        return taken

    raw, q_slabs, do_slabs = take(2), take(lay.group - 1), take(lay.group - 1)
    o_in, stat_in = take(2)
    below, above = take(lay.line - 1), take(lay.line - 1)
    outs, (do_out, stat_out, gq_out) = take(lay.group), take(3)
    to_below, to_above = take(lay.line - 1), take(lay.line - 1)
    q_scr, do_scr, sum_scr, k_tab, v_tab, dk_acc, dv_acc, s_scr, e_scr, m_scr = refs[:10]
    o_acc, o_scr, st_scr, sems = refs[10:]
    u, w = where_ref[0], where_ref[1]
    heads = GROUP_WIDTH
    made = Copies(sems)
    first = lay.place(w)[0]

    def far_base(plane):
        return jnp.where(lay.place(plane)[0] > first, lay.group, 0)

    def far_copies(below, above, into):
        return [
            (
                valid & (lay.place(plane)[0] != first),
                table_copies(lay, made, plane, (k_tab, v_tab), table, into, far_base(plane)),
            )
            for valid, plane, table in offsets(lay, w, below, above)
        ]

    guarded = far_copies(below, above, True)
    loads = {}
    for x in range(lay.group):
        cols = columns(u * heads, heads)
        loads[x] = [
            made.make(q_slabs[x - 1] if x else raw[0].at[:, cols], q_scr.at[x]),
            made.make(do_slabs[x - 1] if x else raw[1].at[:, cols], do_scr.at[x]),
            made.make(o_in.at[x], sum_scr.at[x]),
            made.make(stat_in.at[x], st_scr.at[x]),
        ]
    start_guarded(guarded)
    for some in loads.values():
        start_all(some)
    dk_acc[...] = jnp.zeros_like(dk_acc)
    dv_acc[...] = jnp.zeros_like(dv_acc)
    start_guarded(guarded, wait_all)

    shape = (lay.tokens, HEAD_WIDTH)
    lane = lax.broadcasted_iota(jnp.int32, shape, 1)
    saves = {
        x: [
            made.make(o_scr.at[x % 2], outs[x]),
            made.make(do_scr.at[x], do_out.at[x]),
            made.make(st_scr.at[x], stat_out.at[x]),
            made.make(sum_scr.at[x], gq_out.at[x]),
        ]
        for x in range(lay.group)
    }

    def one(x, carry):
        slot = x % 2
        at_place(x, loads, wait_all)
        at_place(x, {p + 2: some for p, some in saves.items()}, lambda c: wait_all(c[:1]))
        mine = lay.query_block(w, jnp.bitwise_xor(u, x))
        live = count_ref[mine]

        def far(i, run):
            block = lay.table_block(list_ref[mine, i], u)

            @pl.when((block < first) | (block >= first + lay.group))
            def _():
                run(jnp.where(block < first, block, block - lay.group))

        for g in range(heads):
            m_scr[g] = spread(st_scr[x, :, g : g + 1], shape)

        def scores(i, c):
            def run(block):
                for g in range(heads):
                    s = dot(q_scr[x, :, COLS[g]], k_tab[block], NT)
                    s_scr[i - 1, g] = s
                    m_scr[g] = lane_max(m_scr[g], s)

            far(i, run)
            return c

        lax.fori_loop(1, live, scores, 0)
        stats = jnp.zeros(shape, jnp.float32)
        for g in range(heads):
            top = spread(jnp.max(m_scr[g], axis=1, keepdims=True), shape)
            old = spread(st_scr[x, :, g : g + 1], shape)
            total = spread(st_scr[x, :, heads + g : heads + g + 1], shape)
            fade = jnp.exp2((old - top) * EXP2_SCALE)
            o_acc[g, :, :HEAD_WIDTH] = sum_scr[x, :, COLS[g]] * fade
            o_acc[g, :, HEAD_WIDTH:] = total * fade
            m_scr[g] = top
            stats = jnp.where(lane == g, top, stats)

        def weigh(i, c):
            def run(block):
                v_ones = values_and_ones(v_tab[block])
                for g in range(heads):
                    e = score_weights(s_scr[i - 1, g], m_scr[g])
                    e_scr[i - 1, g] = e
                    o_acc[g] += dot(e, v_ones, NN)

            far(i, run)
            return c

        lax.fori_loop(1, live, weigh, 0)
        for g in range(heads):
            inverse = 1.0 / o_acc[g, :, HEAD_WIDTH:]
            attended = (o_acc[g, :, :HEAD_WIDTH] * inverse).astype(jnp.bfloat16)
            o_scr[slot, :, COLS[g]] = attended
            cot = do_scr[x, :, COLS[g]].astype(jnp.float32)
            delta = jnp.sum(attended.astype(jnp.float32) * cot, axis=1, keepdims=True)
            delta = delta * inverse
            m_scr[g] = delta
            stats = jnp.where(lane == heads + g, delta, stats)
            do_scr[x, :, COLS[g]] = (cot * inverse).astype(jnp.bfloat16)
        st_scr[x] = stats
        sum_scr[x] = jnp.zeros(sum_scr.shape[1:], jnp.float32)

        def grads(i, c):
            def run(block):
                dk, dv = None, None
                for g in range(heads):
                    cot = do_scr[x, :, COLS[g]]
                    e = e_scr[i - 1, g]
                    ds = score_grads(e, cot, v_tab[block], m_scr[g])
                    sum_scr[x, :, COLS[g]] += dot(ds, k_tab[block], NN)
                    dk_g = dot(ds, q_scr[x, :, COLS[g]], TN)
                    dv_g = dot(e, cot, TN)
                    dk = dk_g if dk is None else dk + dk_g
                    dv = dv_g if dv is None else dv + dv_g
                dk_acc[block] += dk
                dv_acc[block] += dv

            far(i, run)
            return c

        lax.fori_loop(1, live, grads, 0)
        at_place(x, saves, start_all)
        return carry

    lax.fori_loop(0, lay.group, one, 0)

    def narrow(b, carry):
        k_tab[b] = (dk_acc[b] * SCORE_SCALE).astype(jnp.bfloat16)
        v_tab[b] = dv_acc[b].astype(jnp.bfloat16)
        return carry

    lax.fori_loop(0, k_tab.shape[0], narrow, 0)
    guarded = far_copies(to_below, to_above, False)
    start_guarded(guarded)
    start_guarded(guarded, wait_all)
    for x, some in saves.items():
        wait_all(some if x >= lay.group - 2 else some[1:])


def near_kernel(lay, places, begin, end, list_ref, count_ref, where_ref, *refs):
    refs = list(refs)

    def take(n):
        taken = refs[:n]
        del refs[:n]
        return taken

    near = lay.per_block - 1
    raw = take(1 if begin else 0)
    slabs = take(len(places) - len(raw))
    do_in, stat_in, gq_in = take(3)
    own_table, below, above = take(1)[0], take(near), take(near)
    sums_in = [] if begin else take(2)
    if end:
        take(2 * near)
    outs = take(len(places))
    if end:
        own_sums, to_below, to_above = take(1)[0], take(near), take(near)
    else:
        sums_out = take(2)
    q_scr, do_scr, st_scr, gq_acc, k_tab, v_tab, dk_acc, dv_acc, m_scr, d_scr, sems = refs
    u, w = where_ref[0], where_ref[1]
    heads = GROUP_WIDTH
    made = Copies(sems)
    first = lay.place(w)[0]

    def is_near(valid, plane):
        return valid & (lay.place(plane)[0] == first)

    copies, guarded = near_tables(lay, made, w, (k_tab, v_tab), own_table, below, above)
    loads = {}
    for n, x in enumerate(places):
        if x == 0:
            src = raw[0].at[:, columns(u * heads, heads)]
        else:
            src = slabs[n - len(raw)]
        loads[n] = [
            made.make(src, q_scr.at[n]),
            made.make(do_in.at[x], do_scr.at[n]),
            made.make(stat_in.at[x], st_scr.at[n]),
            made.make(gq_in.at[x], gq_acc.at[n]),
        ]
    if not begin:
        copies += [made.make(sums_in[0], dk_acc), made.make(sums_in[1], dv_acc)]
    start_all(copies)
    start_guarded(guarded)
    for some in loads.values():
        start_all(some)
    if begin:
        dk_acc[...] = jnp.zeros_like(dk_acc)
        dv_acc[...] = jnp.zeros_like(dv_acc)
    wait_all(copies)
    start_guarded(guarded, wait_all)
    saves = {n: [made.make(q_scr.at[n], outs[n])] for n in loads}

    def one(n, carry):
        at_place(n, loads, wait_all)
        mine = lay.query_block(w, jnp.bitwise_xor(u, n + places[0]))
        for g in range(heads):
            m_scr[g] = jnp.broadcast_to(st_scr[n, :, g : g + 1], m_scr.shape[1:])
            d_scr[g] = jnp.broadcast_to(
                st_scr[n, :, heads + g : heads + g + 1], d_scr.shape[1:]
            )

        def grads(i, c):
            block = lay.table_block(list_ref[mine, i], u) - first

            @pl.when((block >= 0) & (block < lay.group))
            def _():
                dk, dv = None, None
                for g in range(heads):
                    q, cot = q_scr[n, :, COLS[g]], do_scr[n, :, COLS[g]]
                    e = score_weights(dot(q, k_tab[block], NT), m_scr[g])
                    ds = score_grads(e, cot, v_tab[block], d_scr[g])
                    gq_acc[n, :, COLS[g]] += dot(ds, k_tab[block], NN)
                    dk_g = dot(ds, q, TN)
                    dv_g = dot(e, cot, TN)
                    dk = dk_g if dk is None else dk + dk_g
                    dv = dv_g if dv is None else dv + dv_g
                dk_acc[block] += dk
                dv_acc[block] += dv

            return c

        lax.fori_loop(0, count_ref[mine], grads, 0)
        for g in range(heads):
            q_scr[n, :, COLS[g]] = (gq_acc[n, :, COLS[g]] * SCORE_SCALE).astype(jnp.bfloat16)
        at_place(n, saves, start_all)
        return carry

    lax.fori_loop(0, len(places), one, 0)
    if end:

        def narrow(b, carry):
            k_tab[b] = (dk_acc[b] * SCORE_SCALE).astype(jnp.bfloat16)
            v_tab[b] = dv_acc[b].astype(jnp.bfloat16)
            return carry

        lax.fori_loop(0, lay.group, narrow, 0)
        copies = table_copies(lay, made, w, (k_tab, v_tab), own_sums, False, first)
        guarded = [
            (is_near(valid, plane), table_copies(lay, made, plane, (k_tab, v_tab), t, False, first))
            for valid, plane, t in offsets(lay, w, to_below, to_above)
        ]
    else:
        copies = [made.make(dk_acc, sums_out[0]), made.make(dv_acc, sums_out[1])]
        guarded = []
    start_all(copies)
    start_guarded(guarded)
    start_guarded(guarded, wait_all)
    wait_all(copies)
    for some in saves.values():
        wait_all(some)


def kernel_call(kernel, lay, scalars, operands, out_shape, scratch, tiles, aliases):
    return pl.pallas_call(
        kernel,
        out_shape=out_shape,
        grid_spec=pltpu.PrefetchScalarGridSpec(
            num_scalar_prefetch=len(scalars),
            grid=(1,),
            in_specs=[ANY] * len(operands),
            out_specs=[ANY] * len(out_shape),
            scratch_shapes=scratch,
        ),
        input_output_aliases=aliases,
        compiler_params=pltpu.CompilerParams(vmem_limit_bytes=VMEM_BYTES),
        cost_estimate=pl.CostEstimate(
            flops=tiles * 24 * lay.tokens * BLOCK_TOKENS * HEAD_WIDTH * GROUP_WIDTH,
            transcendentals=tiles * lay.tokens * BLOCK_TOKENS * GROUP_WIDTH,
            bytes_accessed=16 * 1024 * 1024,
        ),
    )(*scalars, *operands)


def near_forward(lay, scalars, raw, slabs, own_table, below, above):
    bf, f32 = jnp.bfloat16, jnp.float32
    width = GROUP_WIDTH * HEAD_WIDTH
    near = (lay.group, BLOCK_TOKENS, HEAD_WIDTH)
    own = (lay.group, lay.tokens, width)
    most = scalars[0].shape[1]
    n = lay.per_block - 1
    stats = (lay.group, lay.tokens, HEAD_WIDTH)
    scratch = [
        pltpu.VMEM(own, bf),
        *[pltpu.VMEM(near, bf)] * 2,
        pltpu.VMEM((most, GROUP_WIDTH, lay.tokens, BLOCK_TOKENS), f32),
        pltpu.VMEM((GROUP_WIDTH, lay.tokens, HEAD_WIDTH), f32),
        pltpu.VMEM((GROUP_WIDTH, lay.tokens, 2 * HEAD_WIDTH), f32),
        pltpu.VMEM((2, lay.tokens, width), f32),
        pltpu.VMEM(stats, f32),
        pltpu.SemaphoreType.DMA((3 * lay.group + 4 * n + 2,)),
    ]
    out_shape = [jax.ShapeDtypeStruct(own, f32), jax.ShapeDtypeStruct(stats, f32)]
    operands = [raw, *slabs, own_table, *below[:n], *above[:n]]
    return kernel_call(
        functools.partial(near_forward_kernel, lay),
        lay, scalars, operands, out_shape, scratch, lay.group, {},
    )


def forward(lay, scalars, raw, q_slabs, do_slabs, begun, below, above):
    bf, f32 = jnp.bfloat16, jnp.float32
    width = GROUP_WIDTH * HEAD_WIDTH
    far_tables = (lay.blocks - lay.group, BLOCK_TOKENS, HEAD_WIDTH)
    own = (lay.group, lay.tokens, width)
    most = scalars[0].shape[1]
    tile = (GROUP_WIDTH, lay.tokens, BLOCK_TOKENS)
    far = 2 * (lay.line - 1)
    stats = (lay.group, lay.tokens, HEAD_WIDTH)
    scratch = [
        *[pltpu.VMEM(own, bf)] * 2,
        pltpu.VMEM(own, f32),
        *[pltpu.VMEM(far_tables, bf)] * 2,
        *[pltpu.VMEM(far_tables, f32)] * 2,
        pltpu.VMEM((most - 1, *tile), f32),
        pltpu.VMEM((most - 1, *tile), bf),
        pltpu.VMEM((GROUP_WIDTH, lay.tokens, HEAD_WIDTH), f32),
        pltpu.VMEM((GROUP_WIDTH, lay.tokens, 2 * HEAD_WIDTH), f32),
        pltpu.VMEM((2, lay.tokens, width), bf),
        pltpu.VMEM(stats, f32),
        pltpu.SemaphoreType.DMA((8 * lay.group + 4 * far,)),
    ]
    table = (2, lay.group, lay.tokens, HEAD_WIDTH)
    out_shape = [bf16(lay.tokens, width)] * lay.group
    out_shape += [bf16(*own), jax.ShapeDtypeStruct(stats, f32), jax.ShapeDtypeStruct(own, f32)]
    out_shape += [bf16(*table)] * far
    operands = [*raw, *q_slabs, *do_slabs, *begun, *below, *above]
    outs = kernel_call(
        functools.partial(forward_kernel, lay),
        lay, scalars, operands, out_shape, scratch, lay.group * most // 4, {},
    )
    n = lay.group
    return outs[:n], outs[n : n + 3], outs[n + 3 : n + 2 + lay.line], outs[n + 2 + lay.line :]


def near_grads(lay, scalars, places, raw, slabs, carried, own_table, below, above, sums, to_below, to_above):
    bf, f32 = jnp.bfloat16, jnp.float32
    width = GROUP_WIDTH * HEAD_WIDTH
    n, near = len(places), lay.per_block - 1
    begin, end = places[0] == 0, places[-1] == lay.group - 1
    whole = (lay.group, BLOCK_TOKENS, HEAD_WIDTH)
    scratch = [
        *[pltpu.VMEM((n, lay.tokens, width), bf)] * 2,
        pltpu.VMEM((n, lay.tokens, HEAD_WIDTH), f32),
        pltpu.VMEM((n, lay.tokens, width), f32),
        *[pltpu.VMEM(whole, bf)] * 2,
        *[pltpu.VMEM(whole, f32)] * 2,
        *[pltpu.VMEM((GROUP_WIDTH, lay.tokens, HEAD_WIDTH), f32)] * 2,
        pltpu.SemaphoreType.DMA((5 * n + 8 * near + 8,)),
    ]
    operands = [*(raw if begin else []), *slabs, *carried, own_table, *below[:near], *above[:near], *sums]
    out_shape, aliases = [bf16(lay.tokens, width)] * n, {}
    if end:
        out_shape.append(bf16(2, lay.group, lay.tokens, HEAD_WIDTH))
        for array in (*to_below[:near], *to_above[:near]):
            aliases[len(scalars) + len(operands)] = len(out_shape)
            operands.append(array)
            out_shape.append(bf16(*array.shape))
    else:
        out_shape += [jax.ShapeDtypeStruct(whole, f32)] * 2
    most = scalars[0].shape[1]
    outs = kernel_call(
        functools.partial(near_kernel, lay, places, begin, end),
        lay, scalars, operands, out_shape, scratch, n * most // 4, aliases,
    )
    return outs[:n], outs[n:]


def add(a, b):
    return (a.astype(jnp.float32) + b.astype(jnp.float32)).astype(jnp.bfloat16)


def shards(ctx_size, head_size, queries, keys, values, cotangent, block_list, block_count):
    lay = Layout(ctx_size, head_size, queries.shape[0])
    ctx_rank, head_rank = lax.axis_index("ctx"), lax.axis_index("head")
    u = lax.rem(ctx_rank, lay.group)
    w = ctx_rank // lay.group * lay.heads + head_rank
    where = jnp.stack([u, w]).astype(jnp.int32)
    n = lay.line

    local, *sent = pack(lay, where, (keys, values), 1, range(lay.group))
    came = [lay.swap(s, x) for x, s in zip(lay.others, sent)]
    own_table = collect(lay, [local, *came])
    below, above = [own_table], [own_table]
    for k in range(1, n):
        below.append(lay.shift(below[-1], range(k - 1, n - 1), 1))
        above.append(lay.shift(above[-1], range(1, n - k + 1), -1))
    scalars = (block_list, block_count, where)
    raw = (queries, cotangent)
    sent = pack_one(lay, where, queries, GROUP_WIDTH)
    slabs = [lay.swap(s, x) for x, s in zip(lay.others, sent)]
    sent = pack_one(lay, where, cotangent, GROUP_WIDTH)
    do_slabs = [lay.swap(s, x) for x, s in zip(lay.others, sent)]
    begun = near_forward(lay, scalars, queries, slabs, own_table, below[1:], above[1:])
    outs, carried, to_below, to_above = forward(
        lay, scalars, raw, slabs, do_slabs, begun, below[1:], above[1:]
    )
    attended = [outs[0], *[lay.swap(s, x) for x, s in zip(lay.others, outs[1:])]]
    up, down = to_above[n - 2], to_below[n - 2]
    shares = [list(range(i, i + lay.group // 2)) for i in range(0, lay.group, lay.group // 2)]
    grad_query, sums = [], []
    for k in range(n - 1, 0, -1):
        step = n - k
        up = lay.shift(up, range(0, n - k), 1)
        down = lay.shift(down, range(k, n), -1)
        if step <= len(shares):
            places = shares[step - 1]
            outs, sums = near_grads(
                lay, scalars, places, raw[:1],
                [slabs[x - 1] for x in places if x],
                carried, own_table, below[1:], above[1:], sums, to_below, to_above,
            )
            grad_query += [lay.swap(s, x) if x else s for x, s in zip(places, outs)]
            if step == len(shares):
                near = lay.per_block - 1
                own_sums = sums[0]
                to_below = [*sums[1 : 1 + near], *to_below[near:]]
                to_above = [*sums[1 + near :], *to_above[near:]]
        if k > 1:
            up, down = add(up, to_above[k - 2]), add(down, to_below[k - 2])
    local, *sent = split(lay, [own_sums, up, down])
    came = [lay.swap(s, x) for x, s in zip(lay.others, sent)]
    key_grad, value_grad = unpack(lay, where, [[local, *came]], 1)
    attn_out = unpack(lay, where, [attended], GROUP_WIDTH)[0]
    grad_q = unpack(lay, where, [grad_query], GROUP_WIDTH)[0]
    return attn_out, grad_q, key_grad, value_grad


def solution(mesh):
    placed = P(("ctx", "head"), None)

    def body(*args):
        return shards(mesh.shape["ctx"], mesh.shape["head"], *args)

    return jax.shard_map(
        body,
        mesh=mesh,
        in_specs=(placed,) * 4 + (P(), P()),
        out_specs=(placed,) * 4,
        check_vma=False,
    )
```

```python
import functools
import math

import jax
import jax.numpy as jnp
from jax import lax
from jax.experimental import pallas as pl
from jax.experimental.pallas import tpu as pltpu
from jax.sharding import PartitionSpec as P


QUERY_HEADS = 48
KEY_VALUE_HEADS = 8
HEAD_WIDTH = 128
BLOCK_TOKENS = 512
GROUP_WIDTH = QUERY_HEADS // KEY_VALUE_HEADS

SCORE_SCALE = HEAD_WIDTH ** (-0.5)
EXP2_SCALE = SCORE_SCALE * math.log2(math.e)
LOWEST = -3.0e38
VMEM_BYTES = 62 * 1024 * 1024


NT = (((1,), (1,)), ((), ()))
NN = (((1,), (0,)), ((), ()))
TN = (((0,), (0,)), ((), ()))


def dot(a, b, dims):
    return lax.dot_general(a, b, dims, preferred_element_type=jnp.float32)


def bf16(*shape):
    return jax.ShapeDtypeStruct(shape, jnp.bfloat16)


ANY = pl.BlockSpec(memory_space=pl.ANY)
VMEM = pl.BlockSpec(memory_space=pltpu.VMEM)
SMEM = pl.BlockSpec(memory_space=pltpu.SMEM)


class Copies:
    def __init__(self, sems):
        self.sems, self.made = sems, 0

    def make(self, src, dst):
        self.made += 1
        return pltpu.make_async_copy(src, dst, self.sems.at[self.made - 1])

    @staticmethod
    def run(copies):
        for copy in copies:
            copy.start()
        for copy in copies:
            copy.wait()


class Layout:
    def __init__(self, ctx_size, head_size, tokens):
        self.group = KEY_VALUE_HEADS
        assert ctx_size % self.group == 0
        self.ctx_size, self.heads, self.tokens = ctx_size, head_size, tokens
        self.line = ctx_size // self.group * head_size
        self.per_ctx = tokens * head_size // BLOCK_TOKENS
        self.per_block = BLOCK_TOKENS // tokens
        self.blocks = ctx_size * self.per_ctx
        self.others = range(1, self.group)

    def device(self, w, u):
        m, h = divmod(w, self.heads)
        return (m * self.group + u) * self.heads + h

    def swap(self, value, x):
        pairs = [
            (self.device(w, u), self.device(w, u ^ x))
            for w in range(self.line)
            for u in range(self.group)
        ]
        return lax.ppermute(value, ("ctx", "head"), pairs)

    def shift(self, value, sources, step):
        pairs = [
            (self.device(w, u), self.device(w + step, u)) for w in sources for u in range(self.group)
        ]
        return lax.ppermute(value, ("ctx", "head"), pairs)

    def place(self, w):
        m, h = w // self.heads, w % self.heads
        first = (m * self.per_ctx + h // self.per_block) * self.group
        return first, pl.multiple_of(h % self.per_block * self.tokens, self.tokens)

    def query_block(self, w, u):
        ctx = w // self.heads * self.group + u
        return ctx * self.per_ctx + w % self.heads // self.per_block

    def table_block(self, block, u):
        ctx = block // self.per_ctx
        first = (ctx // self.group * self.per_ctx + block % self.per_ctx) * self.group
        return first + jnp.bitwise_xor(ctx % self.group, u)


def copy_call(body, ins, specs, outs, n, out_spec=ANY):
    def kernel(*refs):
        sems = refs[-1]
        Copies.run(list(body(Copies(sems), refs[: len(ins)], refs[len(ins) : -1])))

    moved = 4 * sum(math.prod(o.shape) for o in outs)
    return pl.pallas_call(
        kernel,
        out_shape=outs,
        in_specs=specs,
        out_specs=[out_spec] * len(outs),
        scratch_shapes=[pltpu.SemaphoreType.DMA((n,))],
        compiler_params=pltpu.CompilerParams(vmem_limit_bytes=VMEM_BYTES),
        cost_estimate=pl.CostEstimate(flops=0, transcendentals=0, bytes_accessed=moved),
    )(*ins)


def columns(index, count=1):
    return pl.ds(pl.multiple_of(index * HEAD_WIDTH, HEAD_WIDTH), count * HEAD_WIDTH)


def pack(lay, u, arrays, count, places):
    def body(copies, ins, outs):
        rank, *raw = ins
        for x, out in zip(places, outs, strict=True):
            cols = columns(jnp.bitwise_xor(rank[0], x) * count, count)
            for half in range(2):
                yield copies.make(raw[half].at[:, cols], out.at[half])

    outs = [bf16(2, lay.tokens, count * HEAD_WIDTH)] * len(places)
    return copy_call(body, [u, *arrays], [SMEM, VMEM, VMEM], outs, 2 * len(places))


def pack_one(lay, u, array, count):
    def body(copies, ins, outs):
        rank, raw = ins
        for x, out in zip(lay.others, outs, strict=True):
            cols = columns(jnp.bitwise_xor(rank[0], x) * count, count)
            yield copies.make(raw.at[:, cols], out)

    outs = [bf16(lay.tokens, count * HEAD_WIDTH)] * len(lay.others)
    return copy_call(body, [u, array], [SMEM, VMEM], outs, len(outs))


def unpack(lay, u, slabs, count):
    flat, plan = [], []
    for out, some in enumerate(slabs):
        for x, part in enumerate(some):
            plan.append((out, x, len(flat)))
            flat.append(part)
    pairs = flat[0].ndim == 3

    def body(copies, ins, outs):
        rank, *parts = ins
        for out, x, at in plan:
            cols = columns(jnp.bitwise_xor(rank[0], x) * count, count)
            if pairs:
                for half in range(2):
                    yield copies.make(parts[at].at[half], outs[half].at[:, cols])
            else:
                yield copies.make(parts[at], outs[out].at[:, cols])

    outs = [bf16(lay.tokens, lay.group * count * HEAD_WIDTH)] * (2 if pairs else len(slabs))
    specs = [SMEM] + [ANY] * len(flat)
    return copy_call(body, [u, *flat], specs, outs, 2 * len(flat), VMEM)


def collect(lay, slabs):
    def body(copies, ins, outs):
        for x, part in enumerate(ins):
            for half in range(2):
                yield copies.make(part.at[half], outs[0].at[half, x])

    outs = [bf16(2, lay.group, lay.tokens, HEAD_WIDTH)]
    specs = [ANY] * lay.group
    return copy_call(body, list(slabs), specs, outs, 2 * lay.group, VMEM)[0]


def split(lay, terms):
    def kernel(*refs):
        ins, outs = refs[: len(terms)], refs[len(terms) :]
        for x, out in enumerate(outs):
            for half in range(2):
                total = ins[0][half, x].astype(jnp.float32)
                for term in ins[1:]:
                    total += term[half, x].astype(jnp.float32)
                out[half] = total.astype(jnp.bfloat16)

    outs = [bf16(2, lay.tokens, HEAD_WIDTH)] * lay.group
    moved = 2 * (len(terms) + 1) * math.prod(terms[0].shape)
    return pl.pallas_call(
        kernel,
        out_shape=outs,
        in_specs=[VMEM] * len(terms),
        out_specs=[VMEM] * len(outs),
        cost_estimate=pl.CostEstimate(flops=0, transcendentals=0, bytes_accessed=moved),
        name="split",
    )(*terms)


def wait_all(copies):
    for copy in copies:
        copy.wait()


def start_all(copies):
    for copy in copies:
        copy.start()


def start_guarded(guarded, run=start_all):
    for valid, some in guarded:

        @pl.when(valid)
        def _():
            run(some)


def at_place(x, lists, run):
    for place, some in lists.items():

        @pl.when(x == place)
        def _():
            run(some)


REPEAT = BLOCK_TOKENS // HEAD_WIDTH
COLS = [pl.ds(g * HEAD_WIDTH, HEAD_WIDTH) for g in range(GROUP_WIDTH)]


def widen(x):
    return jnp.concatenate([x] * REPEAT, axis=1)


def score_weights(s, top):
    return jnp.exp2((s - widen(top)) * EXP2_SCALE).astype(jnp.bfloat16)


def score_grads(e, cot, v, delta):
    return e * (dot(cot, v, NT) - widen(delta)).astype(jnp.bfloat16)


def table_copies(lay, made, plane, refs, table, into, base=0):
    first, row = lay.place(plane)
    part = pl.ds(first - base, lay.group), pl.ds(row, lay.tokens)
    if into:
        return [made.make(table.at[n], ref.at[part]) for n, ref in enumerate(refs)]
    return [made.make(ref.at[part], table.at[n]) for n, ref in enumerate(refs)]


def offsets(lay, w, below, above):
    for k in range(1, len(below) + 1):
        yield w >= k, w - k, below[k - 1]
        yield w + k < lay.line, w + k, above[k - 1]


def near_tables(lay, made, w, refs, own_table, below, above):
    first = lay.place(w)[0]
    guarded = []
    for valid, plane, table in offsets(lay, w, below, above):
        valid = valid & (lay.place(plane)[0] == first)
        guarded.append((valid, table_copies(lay, made, plane, refs, table, True, first)))
    return table_copies(lay, made, w, refs, own_table, True, first), guarded


def lane_max(m, s):
    for part in range(REPEAT):
        m = jnp.maximum(m, s[:, part * HEAD_WIDTH : (part + 1) * HEAD_WIDTH])
    return m


def values_and_ones(v):
    return jnp.concatenate([v, jnp.ones((BLOCK_TOKENS, HEAD_WIDTH), jnp.bfloat16)], axis=1)


def spread(column, shape):
    return jnp.broadcast_to(column, shape)


def near_forward_kernel(lay, list_ref, count_ref, where_ref, *refs):
    refs = list(refs)

    def take(n):
        taken = refs[:n]
        del refs[:n]
        return taken

    near = lay.per_block - 1
    raw, slabs = take(1)[0], take(lay.group - 1)
    own_table, below, above = take(1)[0], take(near), take(near)
    o_out, stat_out = take(2)
    q_scr, k_tab, v_tab, s_scr, m_scr, o_acc, o_scr, st_scr, sems = refs
    u, w = where_ref[0], where_ref[1]
    heads = GROUP_WIDTH
    made = Copies(sems)
    first = lay.place(w)[0]
    copies, guarded = near_tables(lay, made, w, (k_tab, v_tab), own_table, below, above)
    loads = {}
    for x in range(lay.group):
        src = slabs[x - 1] if x else raw.at[:, columns(u * heads, heads)]
        loads[x] = [made.make(src, q_scr.at[x])]
    start_all(copies)
    start_guarded(guarded)
    for some in loads.values():
        start_all(some)
    wait_all(copies)
    start_guarded(guarded, wait_all)
    shape = (lay.tokens, HEAD_WIDTH)
    lane = lax.broadcasted_iota(jnp.int32, shape, 1)
    saves = {
        x: [made.make(o_scr.at[x % 2], o_out.at[x]), made.make(st_scr.at[x], stat_out.at[x])]
        for x in range(lay.group)
    }

    def one(x, carry):
        at_place(x, loads, wait_all)
        at_place(x, {p + 2: some for p, some in saves.items()}, lambda c: wait_all(c[:1]))
        mine = lay.query_block(w, jnp.bitwise_xor(u, x))
        live = count_ref[mine]
        m_scr[...] = jnp.full_like(m_scr, LOWEST)

        def scores(i, c):
            block = lay.table_block(list_ref[mine, i], u) - first

            @pl.when((block >= 0) & (block < lay.group))
            def _():
                for g in range(heads):
                    s = dot(q_scr[x, :, COLS[g]], k_tab[block], NT)
                    s_scr[i, g] = s
                    m_scr[g] = lane_max(m_scr[g], s)

            return c

        lax.fori_loop(0, live, scores, 0)
        for g in range(heads):
            m_scr[g] = spread(jnp.max(m_scr[g], axis=1, keepdims=True), shape)
        o_acc[...] = jnp.zeros_like(o_acc)

        def weigh(i, c):
            block = lay.table_block(list_ref[mine, i], u) - first

            @pl.when((block >= 0) & (block < lay.group))
            def _():
                v_ones = values_and_ones(v_tab[block])
                for g in range(heads):
                    o_acc[g] += dot(score_weights(s_scr[i, g], m_scr[g]), v_ones, NN)

            return c

        lax.fori_loop(0, live, weigh, 0)
        stats = jnp.zeros(shape, jnp.float32)
        for g in range(heads):
            total = o_acc[g, :, HEAD_WIDTH:]
            o_scr[x % 2, :, COLS[g]] = o_acc[g, :, :HEAD_WIDTH] * (1.0 / total)
            stats = jnp.where(lane == g, m_scr[g] + jnp.log(total) / SCORE_SCALE, stats)
        st_scr[x] = stats
        at_place(x, saves, start_all)
        return carry

    lax.fori_loop(0, lay.group, one, 0)
    for x, some in saves.items():
        wait_all(some if x >= lay.group - 2 else some[1:])


def forward_kernel(lay, list_ref, count_ref, where_ref, *refs):
    refs = list(refs)

    def take(n):
        taken = refs[:n]
        del refs[:n]
        return taken

    raw, q_slabs, do_slabs = take(2), take(lay.group - 1), take(lay.group - 1)
    o_in, stat_in = take(2)
    below, above = take(lay.line - 1), take(lay.line - 1)
    outs, (do_out, stat_out, gq_out) = take(lay.group), take(3)
    to_below, to_above = take(lay.line - 1), take(lay.line - 1)
    q_scr, do_scr, sum_scr, k_tab, v_tab, dk_acc, dv_acc, s_scr, e_scr, m_scr = refs[:10]
    o_acc, o_scr, st_scr, begun_scr, sems = refs[10:]
    u, w = where_ref[0], where_ref[1]
    heads = GROUP_WIDTH
    made = Copies(sems)
    first = lay.place(w)[0]

    def far_base(plane):
        return jnp.where(lay.place(plane)[0] > first, lay.group, 0)

    def far_copies(below, above, into):
        return [
            (
                valid & (lay.place(plane)[0] != first),
                table_copies(lay, made, plane, (k_tab, v_tab), table, into, far_base(plane)),
            )
            for valid, plane, table in offsets(lay, w, below, above)
        ]

    guarded = far_copies(below, above, True)
    loads = {}
    for x in range(lay.group):
        cols = columns(u * heads, heads)
        loads[x] = [
            made.make(q_slabs[x - 1] if x else raw[0].at[:, cols], q_scr.at[x]),
            made.make(do_slabs[x - 1] if x else raw[1].at[:, cols], do_scr.at[x]),
            made.make(o_in.at[x], sum_scr.at[x]),
            made.make(stat_in.at[x], st_scr.at[x]),
        ]
    start_guarded(guarded)
    for some in loads.values():
        start_all(some)
    dk_acc[...] = jnp.zeros_like(dk_acc)
    dv_acc[...] = jnp.zeros_like(dv_acc)
    start_guarded(guarded, wait_all)

    shape = (lay.tokens, HEAD_WIDTH)
    lane = lax.broadcasted_iota(jnp.int32, shape, 1)
    saves = {
        x: [
            made.make(o_scr.at[x % 2], outs[x]),
            made.make(do_scr.at[x], do_out.at[x]),
            made.make(st_scr.at[x], stat_out.at[x]),
            made.make(sum_scr.at[x], gq_out.at[x]),
        ]
        for x in range(lay.group)
    }

    def one(x, carry):
        slot = x % 2
        at_place(x, loads, wait_all)
        at_place(x, {p + 2: some for p, some in saves.items()}, lambda c: wait_all(c[:1]))
        mine = lay.query_block(w, jnp.bitwise_xor(u, x))
        live = count_ref[mine]

        def far(i, run):
            block = lay.table_block(list_ref[mine, i], u)

            @pl.when((block < first) | (block >= first + lay.group))
            def _():
                run(jnp.where(block < first, block, block - lay.group))

        for g in range(heads):
            begun = spread(st_scr[x, :, g : g + 1], shape)
            m_scr[g] = begun
            begun_scr[g] = begun

        def scores(i, c):
            def run(block):
                for g in range(heads):
                    s = dot(q_scr[x, :, COLS[g]], k_tab[block], NT)
                    s_scr[i - 1, g] = s
                    m_scr[g] = lane_max(m_scr[g], s)

            far(i, run)
            return c

        lax.fori_loop(1, live, scores, 0)
        stats = jnp.zeros(shape, jnp.float32)
        for g in range(heads):
            top = spread(jnp.max(m_scr[g], axis=1, keepdims=True), shape)
            fade = jnp.exp2((begun_scr[g] - top) * EXP2_SCALE)
            o_acc[g, :, :HEAD_WIDTH] = sum_scr[x, :, COLS[g]] * fade
            o_acc[g, :, HEAD_WIDTH:] = fade
            m_scr[g] = top
            stats = jnp.where(lane == g, top, stats)

        def weigh(i, c):
            def run(block):
                v_ones = values_and_ones(v_tab[block])
                for g in range(heads):
                    e = score_weights(s_scr[i - 1, g], m_scr[g])
                    e_scr[i - 1, g] = e
                    o_acc[g] += dot(e, v_ones, NN)

            far(i, run)
            return c

        lax.fori_loop(1, live, weigh, 0)
        for g in range(heads):
            inverse = 1.0 / o_acc[g, :, HEAD_WIDTH:]
            attended = (o_acc[g, :, :HEAD_WIDTH] * inverse).astype(jnp.bfloat16)
            o_scr[slot, :, COLS[g]] = attended
            cot = do_scr[x, :, COLS[g]].astype(jnp.float32)
            delta = jnp.sum(attended.astype(jnp.float32) * cot, axis=1, keepdims=True)
            delta = delta * inverse
            m_scr[g] = delta
            stats = jnp.where(lane == heads + g, delta, stats)
            do_scr[x, :, COLS[g]] = (cot * inverse).astype(jnp.bfloat16)
        st_scr[x] = stats
        sum_scr[x] = jnp.zeros(sum_scr.shape[1:], jnp.float32)

        def grads(i, c):
            def run(block):
                dk, dv = None, None
                for g in range(heads):
                    cot = do_scr[x, :, COLS[g]]
                    e = e_scr[i - 1, g]
                    ds = score_grads(e, cot, v_tab[block], m_scr[g])
                    sum_scr[x, :, COLS[g]] += dot(ds, k_tab[block], NN)
                    dk_g = dot(ds, q_scr[x, :, COLS[g]], TN)
                    dv_g = dot(e, cot, TN)
                    dk = dk_g if dk is None else dk + dk_g
                    dv = dv_g if dv is None else dv + dv_g
                dk_acc[block] += dk
                dv_acc[block] += dv

            far(i, run)
            return c

        lax.fori_loop(1, live, grads, 0)
        at_place(x, saves, start_all)
        return carry

    lax.fori_loop(0, lay.group, one, 0)

    def narrow(b, carry):
        k_tab[b] = (dk_acc[b] * SCORE_SCALE).astype(jnp.bfloat16)
        v_tab[b] = dv_acc[b].astype(jnp.bfloat16)
        return carry

    lax.fori_loop(0, k_tab.shape[0], narrow, 0)
    guarded = far_copies(to_below, to_above, False)
    start_guarded(guarded)
    start_guarded(guarded, wait_all)
    for x, some in saves.items():
        wait_all(some if x >= lay.group - 2 else some[1:])


def near_kernel(lay, places, begin, end, list_ref, count_ref, where_ref, *refs):
    refs = list(refs)

    def take(n):
        taken = refs[:n]
        del refs[:n]
        return taken

    near = lay.per_block - 1
    raw = take(1 if begin else 0)
    slabs = take(len(places) - len(raw))
    do_in, stat_in, gq_in = take(3)
    own_table, below, above = take(1)[0], take(near), take(near)
    sums_in = [] if begin else take(2)
    if end:
        take(2 * near)
    outs = take(len(places))
    if end:
        own_sums, to_below, to_above = take(1)[0], take(near), take(near)
    else:
        sums_out = take(2)
    q_scr, do_scr, st_scr, gq_acc, k_tab, v_tab, dk_acc, dv_acc, m_scr, d_scr, sems = refs
    u, w = where_ref[0], where_ref[1]
    heads = GROUP_WIDTH
    made = Copies(sems)
    first = lay.place(w)[0]

    def is_near(valid, plane):
        return valid & (lay.place(plane)[0] == first)

    copies, guarded = near_tables(lay, made, w, (k_tab, v_tab), own_table, below, above)
    loads = {}
    for n, x in enumerate(places):
        if x == 0:
            src = raw[0].at[:, columns(u * heads, heads)]
        else:
            src = slabs[n - len(raw)]
        loads[n] = [
            made.make(src, q_scr.at[n]),
            made.make(do_in.at[x], do_scr.at[n]),
            made.make(stat_in.at[x], st_scr.at[n]),
            made.make(gq_in.at[x], gq_acc.at[n]),
        ]
    if not begin:
        copies += [made.make(sums_in[0], dk_acc), made.make(sums_in[1], dv_acc)]
    start_all(copies)
    start_guarded(guarded)
    for some in loads.values():
        start_all(some)
    if begin:
        dk_acc[...] = jnp.zeros_like(dk_acc)
        dv_acc[...] = jnp.zeros_like(dv_acc)
    wait_all(copies)
    start_guarded(guarded, wait_all)
    saves = {n: [made.make(q_scr.at[n], outs[n])] for n in loads}

    def one(n, carry):
        at_place(n, loads, wait_all)
        mine = lay.query_block(w, jnp.bitwise_xor(u, n + places[0]))
        for g in range(heads):
            m_scr[g] = jnp.broadcast_to(st_scr[n, :, g : g + 1], m_scr.shape[1:])
            d_scr[g] = jnp.broadcast_to(
                st_scr[n, :, heads + g : heads + g + 1], d_scr.shape[1:]
            )

        def grads(i, c):
            block = lay.table_block(list_ref[mine, i], u) - first

            @pl.when((block >= 0) & (block < lay.group))
            def _():
                dk, dv = None, None
                for g in range(heads):
                    q, cot = q_scr[n, :, COLS[g]], do_scr[n, :, COLS[g]]
                    e = score_weights(dot(q, k_tab[block], NT), m_scr[g])
                    ds = score_grads(e, cot, v_tab[block], d_scr[g])
                    gq_acc[n, :, COLS[g]] += dot(ds, k_tab[block], NN)
                    dk_g = dot(ds, q, TN)
                    dv_g = dot(e, cot, TN)
                    dk = dk_g if dk is None else dk + dk_g
                    dv = dv_g if dv is None else dv + dv_g
                dk_acc[block] += dk
                dv_acc[block] += dv

            return c

        lax.fori_loop(0, count_ref[mine], grads, 0)
        for g in range(heads):
            q_scr[n, :, COLS[g]] = (gq_acc[n, :, COLS[g]] * SCORE_SCALE).astype(jnp.bfloat16)
        at_place(n, saves, start_all)
        return carry

    lax.fori_loop(0, len(places), one, 0)
    if end:

        def narrow(b, carry):
            k_tab[b] = (dk_acc[b] * SCORE_SCALE).astype(jnp.bfloat16)
            v_tab[b] = dv_acc[b].astype(jnp.bfloat16)
            return carry

        lax.fori_loop(0, lay.group, narrow, 0)
        copies = table_copies(lay, made, w, (k_tab, v_tab), own_sums, False, first)
        guarded = [
            (is_near(valid, plane), table_copies(lay, made, plane, (k_tab, v_tab), t, False, first))
            for valid, plane, t in offsets(lay, w, to_below, to_above)
        ]
    else:
        copies = [made.make(dk_acc, sums_out[0]), made.make(dv_acc, sums_out[1])]
        guarded = []
    start_all(copies)
    start_guarded(guarded)
    start_guarded(guarded, wait_all)
    wait_all(copies)
    for some in saves.values():
        wait_all(some)


def kernel_call(kernel, lay, scalars, operands, out_shape, scratch, tiles, aliases):
    return pl.pallas_call(
        kernel,
        out_shape=out_shape,
        grid_spec=pltpu.PrefetchScalarGridSpec(
            num_scalar_prefetch=len(scalars),
            grid=(1,),
            in_specs=[ANY] * len(operands),
            out_specs=[ANY] * len(out_shape),
            scratch_shapes=scratch,
        ),
        input_output_aliases=aliases,
        compiler_params=pltpu.CompilerParams(vmem_limit_bytes=VMEM_BYTES),
        cost_estimate=pl.CostEstimate(
            flops=tiles * 24 * lay.tokens * BLOCK_TOKENS * HEAD_WIDTH * GROUP_WIDTH,
            transcendentals=tiles * lay.tokens * BLOCK_TOKENS * GROUP_WIDTH,
            bytes_accessed=16 * 1024 * 1024,
        ),
    )(*scalars, *operands)


def near_forward(lay, scalars, raw, slabs, own_table, below, above):
    bf, f32 = jnp.bfloat16, jnp.float32
    width = GROUP_WIDTH * HEAD_WIDTH
    near = (lay.group, BLOCK_TOKENS, HEAD_WIDTH)
    own = (lay.group, lay.tokens, width)
    most = scalars[0].shape[1]
    n = lay.per_block - 1
    stats = (lay.group, lay.tokens, HEAD_WIDTH)
    scratch = [
        pltpu.VMEM(own, bf),
        *[pltpu.VMEM(near, bf)] * 2,
        pltpu.VMEM((most, GROUP_WIDTH, lay.tokens, BLOCK_TOKENS), f32),
        pltpu.VMEM((GROUP_WIDTH, lay.tokens, HEAD_WIDTH), f32),
        pltpu.VMEM((GROUP_WIDTH, lay.tokens, 2 * HEAD_WIDTH), f32),
        pltpu.VMEM((2, lay.tokens, width), f32),
        pltpu.VMEM(stats, f32),
        pltpu.SemaphoreType.DMA((3 * lay.group + 4 * n + 2,)),
    ]
    out_shape = [jax.ShapeDtypeStruct(own, f32), jax.ShapeDtypeStruct(stats, f32)]
    operands = [raw, *slabs, own_table, *below[:n], *above[:n]]
    return kernel_call(
        functools.partial(near_forward_kernel, lay),
        lay, scalars, operands, out_shape, scratch, lay.group, {},
    )


def forward(lay, scalars, raw, q_slabs, do_slabs, begun, below, above):
    bf, f32 = jnp.bfloat16, jnp.float32
    width = GROUP_WIDTH * HEAD_WIDTH
    far_tables = (lay.blocks - lay.group, BLOCK_TOKENS, HEAD_WIDTH)
    own = (lay.group, lay.tokens, width)
    most = scalars[0].shape[1]
    tile = (GROUP_WIDTH, lay.tokens, BLOCK_TOKENS)
    far = 2 * (lay.line - 1)
    stats = (lay.group, lay.tokens, HEAD_WIDTH)
    scratch = [
        *[pltpu.VMEM(own, bf)] * 2,
        pltpu.VMEM(own, f32),
        *[pltpu.VMEM(far_tables, bf)] * 2,
        *[pltpu.VMEM(far_tables, f32)] * 2,
        pltpu.VMEM((most - 1, *tile), f32),
        pltpu.VMEM((most - 1, *tile), bf),
        pltpu.VMEM((GROUP_WIDTH, lay.tokens, HEAD_WIDTH), f32),
        pltpu.VMEM((GROUP_WIDTH, lay.tokens, 2 * HEAD_WIDTH), f32),
        pltpu.VMEM((2, lay.tokens, width), bf),
        pltpu.VMEM(stats, f32),
        pltpu.VMEM((GROUP_WIDTH, lay.tokens, HEAD_WIDTH), f32),
        pltpu.SemaphoreType.DMA((8 * lay.group + 4 * far,)),
    ]
    table = (2, lay.group, lay.tokens, HEAD_WIDTH)
    out_shape = [bf16(lay.tokens, width)] * lay.group
    out_shape += [bf16(*own), jax.ShapeDtypeStruct(stats, f32), jax.ShapeDtypeStruct(own, f32)]
    out_shape += [bf16(*table)] * far
    operands = [*raw, *q_slabs, *do_slabs, *begun, *below, *above]
    outs = kernel_call(
        functools.partial(forward_kernel, lay),
        lay, scalars, operands, out_shape, scratch, lay.group * most // 4, {},
    )
    n = lay.group
    return outs[:n], outs[n : n + 3], outs[n + 3 : n + 2 + lay.line], outs[n + 2 + lay.line :]


def near_grads(lay, scalars, places, raw, slabs, carried, own_table, below, above, sums, to_below, to_above):
    bf, f32 = jnp.bfloat16, jnp.float32
    width = GROUP_WIDTH * HEAD_WIDTH
    n, near = len(places), lay.per_block - 1
    begin, end = places[0] == 0, places[-1] == lay.group - 1
    whole = (lay.group, BLOCK_TOKENS, HEAD_WIDTH)
    scratch = [
        *[pltpu.VMEM((n, lay.tokens, width), bf)] * 2,
        pltpu.VMEM((n, lay.tokens, HEAD_WIDTH), f32),
        pltpu.VMEM((n, lay.tokens, width), f32),
        *[pltpu.VMEM(whole, bf)] * 2,
        *[pltpu.VMEM(whole, f32)] * 2,
        *[pltpu.VMEM((GROUP_WIDTH, lay.tokens, HEAD_WIDTH), f32)] * 2,
        pltpu.SemaphoreType.DMA((5 * n + 8 * near + 8,)),
    ]
    operands = [*(raw if begin else []), *slabs, *carried, own_table, *below[:near], *above[:near], *sums]
    out_shape, aliases = [bf16(lay.tokens, width)] * n, {}
    if end:
        out_shape.append(bf16(2, lay.group, lay.tokens, HEAD_WIDTH))
        for array in (*to_below[:near], *to_above[:near]):
            aliases[len(scalars) + len(operands)] = len(out_shape)
            operands.append(array)
            out_shape.append(bf16(*array.shape))
    else:
        out_shape += [jax.ShapeDtypeStruct(whole, f32)] * 2
    most = scalars[0].shape[1]
    outs = kernel_call(
        functools.partial(near_kernel, lay, places, begin, end),
        lay, scalars, operands, out_shape, scratch, n * most // 4, aliases,
    )
    return outs[:n], outs[n:]


def add(a, b):
    return (a.astype(jnp.float32) + b.astype(jnp.float32)).astype(jnp.bfloat16)


def shards(ctx_size, head_size, queries, keys, values, cotangent, block_list, block_count):
    lay = Layout(ctx_size, head_size, queries.shape[0])
    ctx_rank, head_rank = lax.axis_index("ctx"), lax.axis_index("head")
    u = lax.rem(ctx_rank, lay.group)
    w = ctx_rank // lay.group * lay.heads + head_rank
    where = jnp.stack([u, w]).astype(jnp.int32)
    n = lay.line

    local, *sent = pack(lay, where, (keys, values), 1, range(lay.group))
    came = [lay.swap(s, x) for x, s in zip(lay.others, sent)]
    own_table = collect(lay, [local, *came])
    below, above = [own_table], [own_table]
    for k in range(1, n):
        below.append(lay.shift(below[-1], range(k - 1, n - 1), 1))
        above.append(lay.shift(above[-1], range(1, n - k + 1), -1))
    scalars = (block_list, block_count, where)
    raw = (queries, cotangent)
    sent = pack_one(lay, where, queries, GROUP_WIDTH)
    slabs = [lay.swap(s, x) for x, s in zip(lay.others, sent)]
    sent = pack_one(lay, where, cotangent, GROUP_WIDTH)
    do_slabs = [lay.swap(s, x) for x, s in zip(lay.others, sent)]
    begun = near_forward(lay, scalars, queries, slabs, own_table, below[1:], above[1:])
    outs, carried, to_below, to_above = forward(
        lay, scalars, raw, slabs, do_slabs, begun, below[1:], above[1:]
    )
    attended = [outs[0], *[lay.swap(s, x) for x, s in zip(lay.others, outs[1:])]]
    up, down = to_above[n - 2], to_below[n - 2]
    shares = [list(range(i, i + lay.group // 2)) for i in range(0, lay.group, lay.group // 2)]
    grad_query, sums = [], []
    for k in range(n - 1, 0, -1):
        step = n - k
        up = lay.shift(up, range(0, n - k), 1)
        down = lay.shift(down, range(k, n), -1)
        if step <= len(shares):
            places = shares[step - 1]
            outs, sums = near_grads(
                lay, scalars, places, raw[:1],
                [slabs[x - 1] for x in places if x],
                carried, own_table, below[1:], above[1:], sums, to_below, to_above,
            )
            grad_query += [lay.swap(s, x) if x else s for x, s in zip(places, outs)]
            if step == len(shares):
                near = lay.per_block - 1
                own_sums = sums[0]
                to_below = [*sums[1 : 1 + near], *to_below[near:]]
                to_above = [*sums[1 + near :], *to_above[near:]]
        if k > 1:
            up, down = add(up, to_above[k - 2]), add(down, to_below[k - 2])
    local, *sent = split(lay, [own_sums, up, down])
    came = [lay.swap(s, x) for x, s in zip(lay.others, sent)]
    key_grad, value_grad = unpack(lay, where, [[local, *came]], 1)
    attn_out = unpack(lay, where, [attended], GROUP_WIDTH)[0]
    grad_q = unpack(lay, where, [grad_query], GROUP_WIDTH)[0]
    return attn_out, grad_q, key_grad, value_grad


def solution(mesh):
    placed = P(("ctx", "head"), None)

    def body(*args):
        return shards(mesh.shape["ctx"], mesh.shape["head"], *args)

    return jax.shard_map(
        body,
        mesh=mesh,
        in_specs=(placed,) * 4 + (P(), P()),
        out_specs=(placed,) * 4,
        check_vma=False,
    )
```
